256 devices in a mesh: blk: 32 (over x_lo, z, core), own: 8 (over y, x_hi).
Axes of the slice: x: 4 (x_hi: 2, x_lo: 2; x = x_hi * 2 + x_lo), y: 4, z: 8, core: 2. Of those that a mesh axis runs over, the one named last changes fastest.
Arguments:
- embeddings: bfloat16 [32768, 768], P(('blk', 'own')), may hold values from -320 to 320
- centroids: bfloat16 [16384, 768], P('blk'), may hold values from -4 to 4
- log_weight: float32 [16384], P('blk'), may hold values from -0.5 to 1.6
Outputs:
- new_centroids: float32 [16384, 768], P(('blk', 'own'))
- counts: float32 [16384], P(('blk', 'own'))
- log_norm: float32 [32768], P(('blk', 'own'))
The draws below stay inside these ranges and needn't reach their ends.
All inputs are finite; a program needn't handle non-finite values.
Results may differ from the reference program's by a relative error of at most 0.0015.
Values may be sent and summed in bfloat16 or wider, within the bound.
No kernel may reach another device: no remote copies, remote signals or barrier semaphores. Data moves between devices by JAX's collectives and lax.ppermute only.
A program may use at most 64 MiB of HBM per device.

```python
import math
import jax
import jax.numpy as jnp
from jax import lax

D = 768
K = 16384
ROWS = 32768


def centre_base(key):
    values = jax.random.normal(jax.random.fold_in(key, 101), (K, D), jnp.float32)
    return jnp.clip(values, -4.0, 4.0)


def weight_base(key):
    place = jnp.arange(K, dtype=jnp.float32) / K
    noise = jax.random.uniform(jax.random.fold_in(key, 303), (K,), jnp.float32, -0.5, 0.5)
    return jnp.log(1.0 + 2.0 * place) + noise


def draw_centroids(key, part):
    return centre_base(key).astype(jnp.bfloat16)


def draw_log_weight(key, part):
    return weight_base(key)


def draw_embeddings(key, part):
    values = jax.random.normal(jax.random.fold_in(key, 202), (ROWS, D), jnp.float32)
    values = jnp.clip(values, -5.0, 5.0)
    return values.astype(jnp.bfloat16)


def setup_inputs(seed: int = 0) -> dict:
    arg_keys = jax.random.split(jax.random.key(seed), 4)
    embeddings = draw_embeddings(jax.random.fold_in(arg_keys[3], 71), 0)
    centroids = draw_centroids(jax.random.fold_in(arg_keys[3], 71), 0)
    log_weight = draw_log_weight(jax.random.fold_in(arg_keys[3], 71), 0)
    return dict(embeddings=embeddings, centroids=centroids, log_weight=log_weight)


prior_mass = 1.0

def score_rows(row_block, centroids, half_sq, log_weight, scale_root):
    dots = jnp.dot(row_block, centroids.T, preferred_element_type=jnp.float32)
    return (dots - half_sq[None, :]) / scale_root + log_weight[None, :]

def reference(embeddings, centroids, log_weight):
    row_count = embeddings.shape[0]
    block_len = math.gcd(row_count, 1024)
    centre_vals = centroids.astype(jnp.float32)
    half_sq = 0.5 * lax.optimization_barrier(jnp.sum(centre_vals * centre_vals, axis=1))
    scale_root = math.sqrt(D)
    row_blocks = embeddings.reshape(row_count // block_len, block_len, D)

    def advance(running, row_block):
        weighted, counts = running
        logits = score_rows(row_block, centroids, half_sq, log_weight, scale_root)
        peak_val = lax.optimization_barrier(jnp.max(logits, axis=1))
        mass_sum = lax.optimization_barrier(jnp.sum(jnp.exp(logits - peak_val[:, None]), axis=1))
        log_total = peak_val + jnp.log(mass_sum)
        resp_vals = jnp.exp(logits - log_total[:, None])
        counts = counts + lax.optimization_barrier(jnp.sum(resp_vals, axis=0))
        weighted = weighted + jnp.dot(resp_vals.astype(jnp.bfloat16).T, row_block, preferred_element_type=jnp.float32)
        return ((weighted, counts), log_total)
    start_pair = (jnp.zeros((K, D), jnp.float32), jnp.zeros((K,), jnp.float32))
    (weighted, counts), log_total = lax.scan(advance, start_pair, row_blocks)
    updated = (weighted + prior_mass * centre_vals) / (counts[:, None] + prior_mass)
    return (updated, counts, log_total.reshape(row_count))
```

```python
import functools
import math

import jax
import jax.numpy as jnp
from jax import lax
from jax.experimental import pallas as pl
from jax.experimental.pallas import tpu as pltpu
from jax.sharding import Mesh
from jax.sharding import PartitionSpec as P

prior_mass = 1.0

AXES = ("x_lo", "z", "core", "y", "x_hi")
XS = ("x_lo", "x_hi")
OWNERS = ("x_lo", "y", "x_hi")
NZ, NX = 8, 4
LANES = 128
VMEM = pl.BlockSpec(memory_space=pltpu.VMEM)
KERNEL_VMEM = 48 * 1024 * 1024


def along_z(step):
    return [(i, (i + step) % NZ) for i in range(NZ)]


def along_x(step):
    place = [(x % 2) * 2 + x // 2 for x in range(NX)]
    return [(place[x], place[(x + step) % NX]) for x in range(NX)]


def other_core(array):
    return lax.ppermute(array, "core", [(0, 1), (1, 0)])


def row_of(step):
    z, core = lax.axis_index("z"), lax.axis_index("core")
    first = lax.rem(z + step, NZ) * 2
    return first + core, first + 1 - core


def score_kernel(scale_root, n_parts, *refs):
    parts = refs[:n_parts]
    cent_ref, half_ref, weight_ref, rows_ref, logits_ref, lse_ref = refs[n_parts:]
    at = 0
    for part in parts:
        rows_ref[at : at + part.shape[0], :] = part[...]
        at += part.shape[0]
    rows = rows_ref[...]
    n_cent, tile = cent_ref.shape[0], 256
    peak = None
    for k in range(0, n_cent, tile):
        dots = lax.dot_general(
            cent_ref[k : k + tile, :], rows, (((1,), (1,)), ((), ())),
            preferred_element_type=jnp.float32,
        )
        logits = (dots - half_ref[k : k + tile, :]) * (1.0 / scale_root) + weight_ref[k : k + tile, :]
        logits_ref[k : k + tile, :] = logits
        top = jnp.max(logits, axis=0, keepdims=True)
        peak = top if peak is None else jnp.maximum(peak, top)
    mass = jnp.zeros_like(peak)
    for k in range(0, n_cent, tile):
        mass += jnp.sum(jnp.exp(logits_ref[k : k + tile, :] - peak), axis=0, keepdims=True)
    lse = peak + jnp.log(mass)
    for i in range(at // LANES):
        lse_ref[i : i + 1, :] = lse[:, i * LANES : (i + 1) * LANES]


def score(parts, cents, half_sq, log_weight, scale_root):
    count, depth = sum(p.shape[0] for p in parts), cents.shape[1]
    n_cent = cents.shape[0]
    return pl.pallas_call(
        functools.partial(score_kernel, scale_root, len(parts)),
        out_shape=(
            jax.ShapeDtypeStruct((count, depth), jnp.bfloat16),
            jax.ShapeDtypeStruct((n_cent, count), jnp.float32),
            jax.ShapeDtypeStruct((count // LANES, LANES), jnp.float32),
        ),
        in_specs=[VMEM] * (len(parts) + 3),
        out_specs=(VMEM,) * 3,
        compiler_params=pltpu.CompilerParams(vmem_limit_bytes=KERNEL_VMEM),
        cost_estimate=pl.CostEstimate(
            flops=2 * n_cent * count * depth,
            bytes_accessed=2 * (n_cent + 2 * count) * depth + 4 * n_cent * count,
            transcendentals=n_cent * count,
        ),
        name="score",
    )(*parts, cents, half_sq, log_weight)


STEPS = [(0,), (NZ - 1, 1), (NZ - 2, 2), (NZ - 3, 3), (4,)]


def table_kernel(*refs):
    table_ref = refs[-1]
    for dists, lse in zip(STEPS, refs[:-1]):
        for i, dist in enumerate(dists):
            mine, other = row_of(dist)
            table_ref[pl.ds(mine, 1), :] = lse[i : i + 1, :]
            table_ref[pl.ds(other, 1), :] = lse[len(dists) + i : len(dists) + i + 1, :]


def table_of(lses):
    return pl.pallas_call(
        table_kernel,
        out_shape=jax.ShapeDtypeStruct((2 * NZ, LANES), jnp.float32),
        in_specs=[VMEM] * len(lses),
        out_specs=VMEM,
        name="row_table",
    )(*lses)


def joined(*tables):
    top = functools.reduce(jnp.maximum, tables)
    return top + jnp.log(sum(jnp.exp(t - top) for t in tables))


def spread_kernel(*refs):
    n = len(STEPS)
    logits, rows = refs[:n], refs[n : 2 * n]
    norm_ref, sums_ref, counts_ref, own_ref = refs[2 * n :]
    total, count = None, None
    for dists, logits_ref, rows_ref in zip(STEPS, logits, rows):
        resp = []
        order = [row_of(dist) for dist in dists]
        order = [o[0] for o in order] + [o[1] for o in order]
        for i, at in enumerate(order):
            norm = norm_ref[pl.ds(at, 1), :]
            r = jnp.exp(logits_ref[:, i * LANES : (i + 1) * LANES] - norm)
            count = r if count is None else count + r
            resp.append(r.astype(jnp.bfloat16))
        part = jnp.dot(
            jnp.concatenate(resp, axis=1), rows_ref[...], preferred_element_type=jnp.float32
        )
        total = part if total is None else total + part
    sums_ref[...] = total
    counts_ref[...] = jnp.sum(count, axis=1, keepdims=True)
    own_ref[...] = norm_ref[pl.ds(row_of(0)[0], 1), :]


def spread(logits, rows, norm, tile=256):
    n_cent, depth = logits[0].shape[0], rows[0].shape[1]
    n_rows = sum(r.shape[0] for r in rows)
    whole = lambda a: pl.BlockSpec(a.shape, lambda k: (0, 0))
    return pl.pallas_call(
        spread_kernel,
        grid=(n_cent // tile,),
        out_shape=(
            jax.ShapeDtypeStruct((n_cent, depth), jnp.float32),
            jax.ShapeDtypeStruct((n_cent, 1), jnp.float32),
            jax.ShapeDtypeStruct((1, LANES), jnp.float32),
        ),
        in_specs=[pl.BlockSpec((tile, l.shape[1]), lambda k: (k, 0)) for l in logits]
        + [whole(r) for r in rows]
        + [whole(norm)],
        out_specs=(
            pl.BlockSpec((tile, depth), lambda k: (k, 0)),
            pl.BlockSpec((tile, 1), lambda k: (k, 0)),
            pl.BlockSpec((1, LANES), lambda k: (0, 0)),
        ),
        compiler_params=pltpu.CompilerParams(vmem_limit_bytes=KERNEL_VMEM),
        cost_estimate=pl.CostEstimate(
            flops=2 * n_cent * n_rows * depth,
            bytes_accessed=4 * n_cent * n_rows + 2 * n_rows * depth + 4 * n_cent * depth,
            transcendentals=n_cent * n_rows,
        ),
        name="spread",
    )(*logits, *rows, norm)


def gathered_steps(own):
    half = own.shape[0] // 2
    up = down = own
    yield [own, other_core(own)]
    for _ in range(3):
        up = lax.ppermute(up, "z", along_z(1))
        down = lax.ppermute(down, "z", along_z(-1))
        yield [up, down, other_core(jnp.concatenate([up, down]))]
    far = jnp.concatenate(
        [
            lax.ppermute(up[:half], "z", along_z(1)),
            lax.ppermute(down[half:], "z", along_z(-1)),
        ]
    )
    yield [far, other_core(far)]


def local(embeddings, centroids, log_weight):
    local_count, feat_dim = centroids.shape
    scale_root = math.sqrt(feat_dim)
    x_lo = lax.axis_index("x_lo")
    half = local_count // 2
    beside = jnp.concatenate(
        [
            lax.ppermute(centroids[:half], XS, along_x(1)),
            lax.ppermute(centroids[half:], XS, along_x(-1)),
        ]
    )
    weight_beside = lax.ppermute(log_weight, "x_lo", [(0, 1), (1, 0)])

    def in_order(mine, other):
        return jnp.where(x_lo == 0, jnp.concatenate([mine, other]), jnp.concatenate([other, mine]))

    cents = in_order(centroids, beside)
    weight = in_order(log_weight, weight_beside)[:, None]
    wide = cents.astype(jnp.float32)
    half_sq = 0.5 * jnp.sum(wide * wide, axis=1, keepdims=True)

    rows, logits, lses = zip(
        *(score(parts, cents, half_sq, weight, scale_root) for parts in gathered_steps(embeddings))
    )
    table = table_of(lses)
    table = joined(table, other_core(table))
    table = joined(table, lax.ppermute(table, "z", along_z(1)))
    table = joined(table, *(lax.ppermute(table, "z", along_z(s)) for s in (2, -2, 4)))

    sums, counts, log_norm = spread(logits, rows, table)
    low = jnp.maximum(jnp.max(jnp.abs(sums), axis=1, keepdims=True) * 2.0**-14, 2.0**-14)
    low = low.astype(jnp.float16)
    count_high = counts.astype(jnp.float16)
    count_rest = ((counts - count_high.astype(jnp.float32)) * 2.0**11).astype(jnp.float16)
    packed = jnp.concatenate(
        [
            (sums / low.astype(jnp.float32)).astype(jnp.float16),
            jnp.broadcast_to(low, (2 * local_count, 1)),
            count_high,
            count_rest,
            jnp.zeros((2 * local_count, LANES - 3), jnp.float16),
        ],
        axis=1,
    )
    owned = local_count // 8
    came = lax.all_to_all(packed.reshape(16, owned, -1), OWNERS, 0, 0, tiled=True)
    came = came.astype(jnp.float32)
    weighted = jnp.sum(came[:, :, :feat_dim] * came[:, :, feat_dim : feat_dim + 1], axis=0)
    counts = jnp.sum(came[:, :, feat_dim + 1] + came[:, :, feat_dim + 2] * 2.0**-11, axis=0)
    own_index = lax.axis_index(("y", "x_hi"))
    own_centres = lax.dynamic_slice_in_dim(centroids, own_index * owned, owned, 0).astype(jnp.float32)
    updated = (weighted + prior_mass * own_centres) / (counts[:, None] + prior_mass)
    return (updated, counts, log_norm.reshape(-1))


def solution(mesh):
    split = Mesh(mesh.devices.reshape(2, NZ, 2, 4, 2), AXES)
    block = ("x_lo", "z", "core")
    return jax.shard_map(
        local,
        mesh=split,
        in_specs=(P(AXES, None), P(block, None), P(block)),
        out_specs=(P(AXES, None), P(AXES), P(AXES)),
        check_vma=False,
    )
```

```python
import functools
import math

import jax
import jax.numpy as jnp
from jax import lax
from jax.experimental import pallas as pl
from jax.experimental.pallas import tpu as pltpu
from jax.sharding import Mesh
from jax.sharding import PartitionSpec as P

prior_mass = 1.0

AXES = ("x_lo", "z", "core", "y", "x_hi")
XS = ("x_lo", "x_hi")
OWNERS = ("x_lo", "y", "x_hi")
NZ, NX, N_OWNERS = 8, 4, 16
LANES = 128
VMEM = pl.BlockSpec(memory_space=pltpu.VMEM)
EXTRA = 8


def along_z(step):
    return [(i, (i + step) % NZ) for i in range(NZ)]


def along_x(step):
    place = [(x % 2) * 2 + x // 2 for x in range(NX)]
    return [(place[x], place[(x + step) % NX]) for x in range(NX)]


def other_core(array):
    return lax.ppermute(array, "core", [(0, 1), (1, 0)])


def call(kernel, outs, args, name, flops=0, transcendentals=0, vmem=24):
    size = sum(a.size * a.dtype.itemsize for a in (*args, *outs))
    return pl.pallas_call(
        kernel,
        out_shape=outs,
        in_specs=[VMEM] * len(args),
        out_specs=(VMEM,) * len(outs),
        compiler_params=pltpu.CompilerParams(vmem_limit_bytes=vmem * 1024 * 1024),
        cost_estimate=pl.CostEstimate(
            flops=flops, bytes_accessed=size, transcendentals=transcendentals
        ),
        name=name,
    )(*args)


def shape(dims, dtype=jnp.float32):
    return jax.ShapeDtypeStruct(dims, dtype)


def column(row):
    n = row.shape[1]
    return jnp.concatenate(
        [jnp.broadcast_to(row[:, i : i + LANES], (LANES, LANES)).T[:, :1] for i in range(0, n, LANES)]
    )


def centroid_kernel(scale_root, mine_ref, up_ref, down_ref, weight_ref, beside_ref, cent_ref, bias_ref):
    n = mine_ref.shape[0]
    x_lo = lax.axis_index("x_lo")
    first, second = pl.multiple_of(x_lo * n, n), pl.multiple_of((1 - x_lo) * n, n)
    beside = jnp.concatenate([up_ref[...], down_ref[...]])
    for at, block, weight in ((first, mine_ref[...], weight_ref), (second, beside, beside_ref)):
        cent_ref[pl.ds(at, n), :] = block
        wide = block.astype(jnp.float32)
        half_sq = 0.5 * jnp.sum(wide * wide, axis=1, keepdims=True)
        bias_ref[pl.ds(at, n), :] = column(weight[...]) - half_sq * (1.0 / scale_root)


def row_of(step):
    z, core = lax.axis_index("z"), lax.axis_index("core")
    first = lax.rem(z + step, NZ) * 2
    return first + core, first + 1 - core


def score_kernel(scale_root, n_parts, *refs):
    parts = refs[:n_parts]
    cent_ref, bias_ref, rows_ref, logits_ref, lse_ref = refs[n_parts:]
    at = 0
    for part in parts:
        rows_ref[at : at + part.shape[0], :] = part[...]
        at += part.shape[0]
    tile = 256
    for k in range(0, at, tile):
        dots = lax.dot_general(
            cent_ref[...], rows_ref[k : k + tile, :], (((1,), (1,)), ((), ())),
            preferred_element_type=jnp.float32,
        )
        logits = dots * (1.0 / scale_root) + bias_ref[...]
        logits_ref[:, k : k + tile] = logits
        peak = jnp.max(logits, axis=0, keepdims=True)
        lse = peak + jnp.log(jnp.sum(jnp.exp(logits - peak), axis=0, keepdims=True))
        for i in range(tile // LANES):
            row = k // LANES + i
            lse_ref[row : row + 1, :] = lse[:, i * LANES : (i + 1) * LANES]


def score(parts, cents, bias, scale_root):
    count, depth = sum(p.shape[0] for p in parts), cents.shape[1]
    n_cent = cents.shape[0]
    return call(
        functools.partial(score_kernel, scale_root, len(parts)),
        (
            shape((count, depth), jnp.bfloat16),
            shape((n_cent, count)),
            shape((count // LANES, LANES)),
        ),
        (*parts, cents, bias),
        "score",
        2 * n_cent * count * depth,
        n_cent * count,
    )


def table_kernel(orders, *refs):
    table_ref = refs[-1]
    for order, lse in zip(orders, refs[:-1]):
        for i, (dist, side) in enumerate(order):
            table_ref[pl.ds(row_of(dist)[side], 1), :] = lse[i : i + 1, :]


def joined(*tables):
    top = functools.reduce(jnp.maximum, tables)
    return top + jnp.log(sum(jnp.exp(t - top) for t in tables))


def spread_kernel(orders, *refs):
    n = len(orders)
    logits, rows = refs[:n], refs[n : 2 * n]
    norm_ref, packed_ref, own_ref = refs[2 * n :]
    n_cent, depth, tile = logits[0].shape[0], rows[0].shape[1], 256
    owned = n_cent // N_OWNERS
    for k in range(0, n_cent, tile):
        total, count = None, None
        for order, logits_ref, rows_ref in zip(orders, logits, rows):
            resp = []
            for i, (dist, side) in enumerate(order):
                norm = norm_ref[pl.ds(row_of(dist)[side], 1), :]
                r = jnp.exp(logits_ref[k : k + tile, i * LANES : (i + 1) * LANES] - norm)
                count = r if count is None else count + r
                resp.append(r.astype(jnp.bfloat16))
            part = jnp.dot(
                jnp.concatenate(resp, axis=1), rows_ref[...], preferred_element_type=jnp.float32
            )
            total = part if total is None else total + part
        count = jnp.sum(count, axis=1, keepdims=True)
        top = jnp.max(jnp.abs(total), axis=1, keepdims=True)
        scale = jnp.maximum(top * 2.0**-14, 2.0**-14).astype(jnp.bfloat16).astype(jnp.float32)
        total = total * (1.0 / scale)
        high = count.astype(jnp.bfloat16).astype(jnp.float32)
        middle = (count - high).astype(jnp.bfloat16).astype(jnp.float32)
        low = count - high - middle
        lane = lax.broadcasted_iota(jnp.int32, (tile, LANES), 1)
        extra = jnp.zeros((tile, LANES), jnp.float32)
        for i, value in enumerate((scale, high, middle * 2.0**8, low * 2.0**16)):
            extra = jnp.where(lane == i, value, extra)
        extra = extra.T[:EXTRA, :]
        for b in range(tile // owned):
            owner = k // owned + b
            for j in range(depth // LANES):
                packed_ref[owner, j * owned : (j + 1) * owned, :] = total[
                    b * owned : (b + 1) * owned, j * LANES : (j + 1) * LANES
                ]
            at = depth // LANES * owned
            packed_ref[owner, at : at + EXTRA, :] = jnp.concatenate(
                [
                    extra[:, b * owned : (b + 1) * owned],
                    jnp.zeros((EXTRA, LANES - owned), jnp.float32),
                ],
                axis=1,
            )
    own_ref[...] = norm_ref[pl.ds(row_of(0)[0], 1), :]


def update_kernel(came_ref, cent_ref, updated_ref, counts_ref):
    owned, depth = updated_ref.shape
    at = depth // LANES * owned
    extra = jnp.concatenate([came_ref[i, at : at + EXTRA, :] for i in range(N_OWNERS)])
    counts = None
    for i in range(N_OWNERS):
        e = i * EXTRA
        c = extra[e + 1 : e + 2] + (extra[e + 2 : e + 3] * 2.0**-8 + extra[e + 3 : e + 4] * 2.0**-16)
        counts = c if counts is None else counts + c
    counts_ref[...] = counts[:, :owned]
    turned = extra.T
    mass = jnp.broadcast_to(counts, (LANES, LANES)).T[:owned, :1] + prior_mass
    first = lax.axis_index("y") * 2 + lax.axis_index("x_hi")
    own = cent_ref[pl.ds(pl.multiple_of(first * owned, owned), owned), :].astype(jnp.float32)
    for j in range(depth // LANES):
        total = None
        for i in range(N_OWNERS):
            scale = turned[:owned, i * EXTRA : i * EXTRA + 1]
            part = came_ref[i, j * owned : (j + 1) * owned, :] * scale
            total = part if total is None else total + part
        here = slice(j * LANES, (j + 1) * LANES)
        updated_ref[:, here] = (total + prior_mass * own[:, here]) / mass


def local(embeddings, centroids, log_weight):
    local_count, feat_dim = centroids.shape
    n_rows = embeddings.shape[0]
    scale_root = math.sqrt(feat_dim)
    half = local_count // 2
    owned = local_count // 8

    other = other_core(embeddings)
    beside = (
        lax.ppermute(centroids[:half], XS, along_x(1)),
        lax.ppermute(centroids[half:], XS, along_x(-1)),
    )
    weight = log_weight[None, :]
    weight_beside = lax.ppermute(weight, "x_lo", [(0, 1), (1, 0)])
    cents, bias = call(
        functools.partial(centroid_kernel, scale_root),
        (shape((2 * local_count, feat_dim), jnp.bfloat16), shape((2 * local_count, 1))),
        (centroids, *beside, weight, weight_beside),
        "centroid_blocks",
        4 * local_count * feat_dim,
    )

    waiting, order = [embeddings, other], [(0, 0), (0, 1)]
    orders, scored = [], []
    up = down = embeddings
    for step in range(1, 4):
        up = lax.ppermute(up, "z", along_z(1))
        down = lax.ppermute(down, "z", along_z(-1))
        if step > 1:
            scored.append(score(waiting, cents, bias, scale_root))
            orders.append(order)
            up, down, _ = lax.optimization_barrier((up, down, scored[-1][2]))
            waiting, order = [], []
        if step == 2:
            waiting += swapped
            order += [(NZ - 1, 1), (1, 1)]
        if step == 3:
            waiting += swapped
            order += [(NZ - 2, 1), (2, 1)]
        waiting += [up, down]
        order += [(NZ - step, 0), (step, 0)]
        swapped = [other_core(up), other_core(down)]
    piece = n_rows // 2
    far = [
        lax.ppermute(up[:piece], "z", along_z(1)),
        lax.ppermute(down[piece:], "z", along_z(-1)),
    ]
    scored.append(score(waiting, cents, bias, scale_root))
    orders.append(order)
    scored.append(score(swapped, cents, bias, scale_root))
    orders.append([(NZ - 3, 1), (3, 1)])
    far = lax.optimization_barrier((*far, scored[-2][2], scored[-1][2]))[:2]
    far_other = other_core(jnp.concatenate(far))
    scored.append(score([*far, far_other], cents, bias, scale_root))
    orders.append([(4, 0), (4, 1)])
    rows, logits, lses = zip(*scored)

    (table,) = call(
        functools.partial(table_kernel, orders), (shape((2 * NZ, LANES)),), lses, "row_table"
    )
    table = joined(table, other_core(table))
    table = joined(table, lax.ppermute(table, "z", along_z(1)))
    table = joined(table, *(lax.ppermute(table, "z", along_z(s)) for s in (2, -2, 4)))

    n_all = 2 * NZ * n_rows
    packed, log_norm = call(
        functools.partial(spread_kernel, orders),
        (
            shape((N_OWNERS, owned * feat_dim // LANES + EXTRA, LANES)),
            shape((1, LANES)),
        ),
        (*logits, *rows, table),
        "spread",
        4 * local_count * n_all * feat_dim,
        2 * local_count * n_all,
    )
    came = lax.all_to_all(packed.astype(jnp.float16), OWNERS, 0, 0, tiled=True)
    updated, counts = call(
        update_kernel,
        (shape((owned, feat_dim)), shape((1, owned))),
        (came.astype(jnp.float32), centroids),
        "update",
    )
    return (updated, counts.reshape(-1), log_norm.reshape(-1))


def solution(mesh):
    split = Mesh(mesh.devices.reshape(2, NZ, 2, 4, 2), AXES)
    block = ("x_lo", "z", "core")
    return jax.shard_map(
        local,
        mesh=split,
        in_specs=(P(AXES, None), P(block, None), P(block)),
        out_specs=(P(AXES, None), P(AXES), P(AXES)),
        check_vma=False,
    )
```

```python
import functools
import math

import jax
import jax.numpy as jnp
from jax import lax
from jax.experimental import pallas as pl
from jax.experimental.pallas import tpu as pltpu
from jax.sharding import Mesh
from jax.sharding import PartitionSpec as P

prior_mass = 1.0

AXES = ("x_lo", "z", "core", "y", "x_hi")
OWNERS = ("x_lo", "y", "x_hi")
NZ, N_OWNERS = 8, 16
LANES = 128
VMEM = pl.BlockSpec(memory_space=pltpu.VMEM)
EXTRA = 8


def along_z(step):
    return [(i, (i + step) % NZ) for i in range(NZ)]


def other_core(array):
    return lax.ppermute(array, "core", [(0, 1), (1, 0)])


def call(kernel, outs, args, name, flops=0, transcendentals=0, share=1, vmem=24):
    size = sum(a.size * a.dtype.itemsize for a in (*args, *outs)) // share
    return pl.pallas_call(
        kernel,
        out_shape=outs,
        in_specs=[VMEM] * len(args),
        out_specs=(VMEM,) * len(outs),
        compiler_params=pltpu.CompilerParams(vmem_limit_bytes=vmem * 1024 * 1024),
        cost_estimate=pl.CostEstimate(
            flops=flops // share, bytes_accessed=size, transcendentals=transcendentals // share
        ),
        name=name,
    )(*args)


def shape(dims, dtype=jnp.float32):
    return jax.ShapeDtypeStruct(dims, dtype)


def column(row):
    n = row.shape[1]
    return jnp.concatenate(
        [jnp.broadcast_to(row[:, i : i + LANES], (LANES, LANES)).T[:, :1] for i in range(0, n, LANES)]
    )


def centroid_kernel(scale_root, mine_ref, weight_ref, other_ref, other_weight_ref, cent_ref, bias_ref):
    n = mine_ref.shape[0]
    x_lo = lax.axis_index("x_lo")
    for at, block_ref, row_ref in (
        (x_lo, mine_ref, weight_ref),
        (1 - x_lo, other_ref, other_weight_ref),
    ):
        here = pl.ds(pl.multiple_of(at * n, n), n)
        cent_ref[here, :] = block_ref[...]
        wide = block_ref[...].astype(jnp.float32)
        half_sq = 0.5 * jnp.sum(wide * wide, axis=1, keepdims=True)
        bias_ref[here, :] = column(row_ref[...]) - half_sq * (1.0 / scale_root)


def row_of(step):
    z, core = lax.axis_index("z"), lax.axis_index("core")
    first = lax.rem(z + step, NZ) * 2
    return first + core, first + 1 - core


def score_kernel(scale_root, n_parts, *refs):
    parts = refs[:n_parts]
    cent_ref, bias_ref, rows_ref, logits_ref, lse_ref = refs[n_parts:]
    at = 0
    for part in parts:
        rows_ref[at : at + part.shape[0], :] = part[...]
        at += part.shape[0]
    tile = 256
    for k in range(0, at, tile):
        dots = lax.dot_general(
            cent_ref[...], rows_ref[k : k + tile, :], (((1,), (1,)), ((), ())),
            preferred_element_type=jnp.float32,
        )
        logits = dots * (1.0 / scale_root) + bias_ref[...]
        logits_ref[:, k : k + tile] = logits
        peak = jnp.max(logits, axis=0, keepdims=True)
        lse = peak + jnp.log(jnp.sum(jnp.exp(logits - peak), axis=0, keepdims=True))
        for i in range(tile // LANES):
            row = k // LANES + i
            lse_ref[row : row + 1, :] = lse[:, i * LANES : (i + 1) * LANES]


def score(parts, cents, bias, scale_root):
    count, depth = sum(p.shape[0] for p in parts), cents.shape[1]
    n_cent = cents.shape[0]
    return call(
        functools.partial(score_kernel, scale_root, len(parts)),
        (
            shape((count, depth), jnp.bfloat16),
            shape((n_cent, count)),
            shape((count // LANES, LANES)),
        ),
        (*parts, cents, bias),
        "score",
        2 * n_cent * count * depth,
        n_cent * count,
        4,
    )


def table_kernel(orders, *refs):
    table_ref = refs[-1]
    for order, lse in zip(orders, refs[:-1]):
        for i, (dist, side) in enumerate(order):
            table_ref[pl.ds(row_of(dist)[side], 1), :] = lse[i : i + 1, :]


def joined(*tables):
    top = functools.reduce(jnp.maximum, tables)
    return top + jnp.log(sum(jnp.exp(t - top) for t in tables))


def spread_kernel(orders, *refs):
    n = len(orders)
    logits, rows = refs[:n], refs[n : 2 * n]
    norm_ref, packed_ref, own_ref = refs[2 * n :]
    n_cent, depth, tile = logits[0].shape[0], rows[0].shape[1], 256
    owned = n_cent // N_OWNERS
    for k in range(0, n_cent, tile):
        total, count = None, None
        for order, logits_ref, rows_ref in zip(orders, logits, rows):
            resp = []
            for i, (dist, side) in enumerate(order):
                norm = norm_ref[pl.ds(row_of(dist)[side], 1), :]
                r = jnp.exp(logits_ref[k : k + tile, i * LANES : (i + 1) * LANES] - norm)
                count = r if count is None else count + r
                resp.append(r.astype(jnp.bfloat16))
            part = jnp.dot(
                jnp.concatenate(resp, axis=1), rows_ref[...], preferred_element_type=jnp.float32
            )
            total = part if total is None else total + part
        count = jnp.sum(count, axis=1, keepdims=True)
        top = jnp.max(jnp.abs(total), axis=1, keepdims=True)
        scale = jnp.maximum(top * 2.0**-14, 2.0**-14).astype(jnp.bfloat16).astype(jnp.float32)
        total = total * (1.0 / scale)
        high = count.astype(jnp.bfloat16).astype(jnp.float32)
        middle = (count - high).astype(jnp.bfloat16).astype(jnp.float32)
        low = count - high - middle
        lane = lax.broadcasted_iota(jnp.int32, (tile, LANES), 1)
        extra = jnp.zeros((tile, LANES), jnp.float32)
        for i, value in enumerate((scale, high, middle * 2.0**8, low * 2.0**16)):
            extra = jnp.where(lane == i, value, extra)
        extra = extra.T[:EXTRA, :]
        for b in range(tile // owned):
            owner = k // owned + b
            for j in range(depth // LANES):
                packed_ref[owner, j * owned : (j + 1) * owned, :] = total[
                    b * owned : (b + 1) * owned, j * LANES : (j + 1) * LANES
                ]
            at = depth // LANES * owned
            packed_ref[owner, at : at + EXTRA, :] = jnp.concatenate(
                [
                    extra[:, b * owned : (b + 1) * owned],
                    jnp.zeros((EXTRA, LANES - owned), jnp.float32),
                ],
                axis=1,
            )
    own_ref[...] = norm_ref[pl.ds(row_of(0)[0], 1), :]


def update_kernel(came_ref, cent_ref, updated_ref, counts_ref):
    owned, depth = updated_ref.shape
    at = depth // LANES * owned
    extra = jnp.concatenate([came_ref[i, at : at + EXTRA, :] for i in range(N_OWNERS)])
    counts = None
    for i in range(N_OWNERS):
        e = i * EXTRA
        c = extra[e + 1 : e + 2] + (extra[e + 2 : e + 3] * 2.0**-8 + extra[e + 3 : e + 4] * 2.0**-16)
        counts = c if counts is None else counts + c
    counts_ref[...] = counts[:, :owned]
    turned = extra.T
    mass = jnp.broadcast_to(counts, (LANES, LANES)).T[:owned, :1] + prior_mass
    first = lax.axis_index("y") * 2 + lax.axis_index("x_hi")
    own = cent_ref[pl.ds(pl.multiple_of(first * owned, owned), owned), :].astype(jnp.float32)
    for j in range(depth // LANES):
        total = None
        for i in range(N_OWNERS):
            scale = turned[:owned, i * EXTRA : i * EXTRA + 1]
            part = came_ref[i, j * owned : (j + 1) * owned, :] * scale
            total = part if total is None else total + part
        here = slice(j * LANES, (j + 1) * LANES)
        updated_ref[:, here] = (total + prior_mass * own[:, here]) / mass


def local(embeddings, centroids, log_weight):
    local_count, feat_dim = centroids.shape
    n_rows = embeddings.shape[0]
    scale_root = math.sqrt(feat_dim)
    owned = local_count // 8

    up = lax.ppermute(embeddings, "z", along_z(1))
    down = lax.ppermute(embeddings, "z", along_z(-1))
    other = other_core(embeddings)
    beside = lax.ppermute(centroids, "x_lo", [(0, 1), (1, 0)])
    weight = log_weight[None, :]
    weight_beside = lax.ppermute(weight, "x_lo", [(0, 1), (1, 0)])

    def blocks(after):
        beside_now, weight_now, _ = lax.optimization_barrier((beside, weight_beside, after))
        return call(
            functools.partial(centroid_kernel, scale_root),
            (shape((2 * local_count, feat_dim), jnp.bfloat16), shape((2 * local_count, 1))),
            (centroids, weight, beside_now, weight_now),
            "centroid_blocks",
            4 * local_count * feat_dim,
            share=4,
        )

    scored, orders = [], []

    def scores(order, *parts):
        scored.append(score(parts, cents, bias, scale_root))
        orders.append(order)
        return scored[-1][2]

    def moved(first, second):
        return lax.ppermute(first, "z", along_z(1)), lax.ppermute(second, "z", along_z(-1))

    def both(step):
        return [(NZ - step, 0), (step, 0), (NZ - step, 1), (step, 1)]

    piece = n_rows // 2
    came = [[embeddings, other, up, down, other_core(up), other_core(down)]]
    for _ in range(2):
        up, down = moved(up, down)
        came.append([up, down, other_core(up), other_core(down)])
        if len(came) == 2:
            cents, bias = blocks(up)
    up, down = moved(up[:piece], down[piece:])
    done = (
        scores([(0, 0), (0, 1), *both(1)], *came[0]),
        scores(both(2), *came[1]),
        scores(both(3), *came[2]),
    )
    up, down, _ = lax.optimization_barrier((up, down, done))
    scores([(4, 0), (4, 1)], up, down, other_core(jnp.concatenate([up, down])))
    rows, logits, lses = zip(*scored)

    (table,) = call(
        functools.partial(table_kernel, orders), (shape((2 * NZ, LANES)),), lses, "row_table"
    )
    table = joined(table, other_core(table))
    tables = jnp.broadcast_to(table, (NZ, *table.shape))
    table = joined(*lax.all_to_all(tables, "z", 0, 0, tiled=True))

    n_all = 2 * NZ * n_rows
    packed, log_norm = call(
        functools.partial(spread_kernel, orders),
        (
            shape((N_OWNERS, owned * feat_dim // LANES + EXTRA, LANES)),
            shape((1, LANES)),
        ),
        (*logits, *rows, table),
        "spread",
        4 * local_count * n_all * feat_dim,
        2 * local_count * n_all,
    )
    came = lax.all_to_all(packed.astype(jnp.float16), OWNERS, 0, 0, tiled=True)
    updated, counts = call(
        update_kernel,
        (shape((owned, feat_dim)), shape((1, owned))),
        (came.astype(jnp.float32), centroids),
        "update",
    )
    return (updated, counts.reshape(-1), log_norm.reshape(-1))


def solution(mesh):
    split = Mesh(mesh.devices.reshape(2, NZ, 2, 4, 2), AXES)
    block = ("x_lo", "z", "core")
    return jax.shard_map(
        local,
        mesh=split,
        in_specs=(P(AXES, None), P(block, None), P(block)),
        out_specs=(P(AXES, None), P(AXES), P(AXES)),
        check_vma=False,
    )
```

```python
import functools
import math

import jax
import jax.numpy as jnp
from jax import lax
from jax.experimental import pallas as pl
from jax.experimental.pallas import tpu as pltpu
from jax.sharding import Mesh
from jax.sharding import PartitionSpec as P

prior_mass = 1.0

AXES = ("x_lo", "z", "core", "y", "x_hi")
PLANE = ("x_lo", "y", "x_hi")
NZ, N_OWNERS = 8, 16
LANES = 128
VMEM = pl.BlockSpec(memory_space=pltpu.VMEM)
EXTRA = 8


def along_z(step):
    return [(i, (i + step) % NZ) for i in range(NZ)]


def in_plane(step_x, step_y):
    place = lambda x, y: (x % 2 * 4 + y % 4) * 2 + x % 4 // 2
    return [
        (place(x, y), place(x + step_x, y + step_y)) for x in range(4) for y in range(4)
    ]


def other_core(array):
    return lax.ppermute(array, "core", [(0, 1), (1, 0)])


def call(kernel, outs, args, name, flops=0, transcendentals=0, share=1, vmem=24):
    size = sum(a.size * a.dtype.itemsize for a in (*args, *outs)) // share
    return pl.pallas_call(
        kernel,
        out_shape=outs,
        in_specs=[VMEM] * len(args),
        out_specs=(VMEM,) * len(outs),
        compiler_params=pltpu.CompilerParams(vmem_limit_bytes=vmem * 1024 * 1024),
        cost_estimate=pl.CostEstimate(
            flops=flops // share, bytes_accessed=size, transcendentals=transcendentals // share
        ),
        name=name,
    )(*args)


def shape(dims, dtype=jnp.float32):
    return jax.ShapeDtypeStruct(dims, dtype)


def column(row):
    n = row.shape[1]
    return jnp.concatenate(
        [jnp.broadcast_to(row[:, i : i + LANES], (LANES, LANES)).T[:, :1] for i in range(0, n, LANES)]
    )


def in_three(value):
    high = value.astype(jnp.bfloat16)
    rest = value - high.astype(jnp.float32)
    middle = rest.astype(jnp.bfloat16)
    return high, middle, (rest - middle.astype(jnp.float32)).astype(jnp.bfloat16)


def parcel_kernel(cent_ref, weight_ref, *parcels):
    half = cent_ref.shape[0] // 2
    for i, parcel_ref in enumerate(parcels):
        here = slice(i * half, (i + 1) * half)
        parcel_ref[:half, :] = cent_ref[here, :]
        row = jnp.concatenate(in_three(weight_ref[:, here]), axis=1)
        parcel_ref[half:, :] = jnp.broadcast_to(row, (EXTRA, row.shape[1]))


def centroid_kernel(scale_root, *refs):
    parcels = refs[:4]
    cent_ref, bias_ref, own_ref = refs[4:]
    half = parcels[0].shape[0] - EXTRA
    x_lo = lax.axis_index("x_lo")
    for i, parcel_ref in enumerate(parcels):
        block = x_lo if i < 2 else 1 - x_lo
        here = pl.ds(pl.multiple_of(block * (2 * half) + i % 2 * half, half), half)
        cent_ref[here, :] = parcel_ref[:half, :]
        wide = parcel_ref[:half, :].astype(jnp.float32)
        half_sq = 0.5 * jnp.sum(wide * wide, axis=1, keepdims=True)
        parts = parcel_ref[half:, :].astype(jnp.float32)[:1]
        weight = parts[:, :half] + parts[:, half : 2 * half] + parts[:, 2 * half :]
        bias_ref[here, :] = column(weight) - half_sq * (1.0 / scale_root)
    owned = own_ref.shape[0]
    first = x_lo * (2 * half) + (lax.axis_index("y") * 2 + lax.axis_index("x_hi")) * owned
    own_ref[...] = cent_ref[pl.ds(pl.multiple_of(first, owned), owned), :].astype(jnp.float32)


def row_of(step):
    z, core = lax.axis_index("z"), lax.axis_index("core")
    first = lax.rem(z + step, NZ) * 2
    return first + core, first + 1 - core


def score_kernel(scale_root, n_parts, *refs):
    parts = refs[:n_parts]
    cent_ref, bias_ref, rows_ref, logits_ref, lse_ref = refs[n_parts:]
    at = 0
    for part in parts:
        rows_ref[at : at + part.shape[0], :] = part[...]
        at += part.shape[0]
    tile = 256
    for k in range(0, at, tile):
        dots = lax.dot_general(
            cent_ref[...], rows_ref[k : k + tile, :], (((1,), (1,)), ((), ())),
            preferred_element_type=jnp.float32,
        )
        logits = dots * (1.0 / scale_root) + bias_ref[...]
        logits_ref[:, k : k + tile] = logits
        peak = jnp.max(logits, axis=0, keepdims=True)
        lse = peak + jnp.log(jnp.sum(jnp.exp(logits - peak), axis=0, keepdims=True))
        for i in range(tile // LANES):
            row = k // LANES + i
            lse_ref[row : row + 1, :] = lse[:, i * LANES : (i + 1) * LANES]


def score(parts, cents, bias, scale_root):
    count, depth = sum(p.shape[0] for p in parts), cents.shape[1]
    n_cent = cents.shape[0]
    return call(
        functools.partial(score_kernel, scale_root, len(parts)),
        (
            shape((count, depth), jnp.bfloat16),
            shape((n_cent, count)),
            shape((count // LANES, LANES)),
        ),
        (*parts, cents, bias),
        "score",
        2 * n_cent * count * depth,
        n_cent * count,
        4,
    )


def table_kernel(orders, *refs):
    table_ref = refs[-1]
    for order, lse in zip(orders, refs[:-1]):
        for i, (dist, side) in enumerate(order):
            table_ref[pl.ds(row_of(dist)[side], 1), :] = lse[i : i + 1, :]


def joined(*tables):
    top = functools.reduce(jnp.maximum, tables)
    return top + jnp.log(sum(jnp.exp(t - top) for t in tables))


def spread_kernel(orders, *refs):
    n = len(orders)
    logits, rows = refs[:n], refs[n : 2 * n]
    norm_ref, packed_ref, own_ref = refs[2 * n :]
    n_cent, depth, tile = logits[0].shape[0], rows[0].shape[1], 512
    owned = n_cent // N_OWNERS
    for k in range(0, n_cent, tile):
        total, count = None, None
        for order, logits_ref, rows_ref in zip(orders, logits, rows):
            resp = []
            for i, (dist, side) in enumerate(order):
                norm = norm_ref[pl.ds(row_of(dist)[side], 1), :]
                r = jnp.exp(logits_ref[k : k + tile, i * LANES : (i + 1) * LANES] - norm)
                count = r if count is None else count + r
                resp.append(r.astype(jnp.bfloat16))
            part = jnp.dot(
                jnp.concatenate(resp, axis=1), rows_ref[...], preferred_element_type=jnp.float32
            )
            total = part if total is None else total + part
        count = jnp.sum(count, axis=1, keepdims=True)
        top = jnp.max(jnp.abs(total), axis=1, keepdims=True)
        scale = jnp.maximum(top * 2.0**-14, 2.0**-14).astype(jnp.bfloat16).astype(jnp.float32)
        total = total * (1.0 / scale)
        high = count.astype(jnp.bfloat16).astype(jnp.float32)
        middle = (count - high).astype(jnp.bfloat16).astype(jnp.float32)
        low = count - high - middle
        lane = lax.broadcasted_iota(jnp.int32, (tile, LANES), 1)
        extra = jnp.zeros((tile, LANES), jnp.float32)
        for i, value in enumerate((scale, high, middle * 2.0**8, low * 2.0**16)):
            extra = jnp.where(lane == i, value, extra)
        extra = extra.T[:EXTRA, :]
        for b in range(tile // owned):
            owner = k // owned + b
            for j in range(depth // LANES):
                packed_ref[owner, j * owned : (j + 1) * owned, :] = total[
                    b * owned : (b + 1) * owned, j * LANES : (j + 1) * LANES
                ]
            at = depth // LANES * owned
            packed_ref[owner, at : at + EXTRA, :] = jnp.concatenate(
                [
                    extra[:, b * owned : (b + 1) * owned],
                    jnp.zeros((EXTRA, LANES - owned), jnp.float32),
                ],
                axis=1,
            )
    own_ref[...] = norm_ref[pl.ds(row_of(0)[0], 1), :]


def update_kernel(came_ref, own_ref, updated_ref, counts_ref):
    owned, depth = updated_ref.shape
    at = depth // LANES * owned
    extra = jnp.concatenate([came_ref[i, at : at + EXTRA, :] for i in range(N_OWNERS)])
    counts = None
    for i in range(N_OWNERS):
        e = i * EXTRA
        c = extra[e + 1 : e + 2] + (extra[e + 2 : e + 3] * 2.0**-8 + extra[e + 3 : e + 4] * 2.0**-16)
        counts = c if counts is None else counts + c
    counts_ref[...] = counts[:, :owned]
    turned = extra.T
    mass = jnp.broadcast_to(counts, (LANES, LANES)).T[:owned, :1] + prior_mass
    for j in range(depth // LANES):
        total = None
        for i in range(N_OWNERS):
            scale = turned[:owned, i * EXTRA : i * EXTRA + 1]
            part = came_ref[i, j * owned : (j + 1) * owned, :] * scale
            total = part if total is None else total + part
        here = slice(j * LANES, (j + 1) * LANES)
        updated_ref[:, here] = (total + prior_mass * own_ref[:, here]) / mass


def local(embeddings, centroids, log_weight):
    local_count, feat_dim = centroids.shape
    n_rows = embeddings.shape[0]
    scale_root = math.sqrt(feat_dim)
    owned = local_count // 8

    up = lax.ppermute(embeddings, "z", along_z(1))
    down = lax.ppermute(embeddings, "z", along_z(-1))
    other = other_core(embeddings)
    half = local_count // 2
    mine = call(
        parcel_kernel,
        (shape((half + EXTRA, feat_dim), jnp.bfloat16),) * 2,
        (centroids, log_weight[None, :]),
        "centroid_parcels",
        share=4,
    )
    beside = (
        lax.ppermute(mine[0], PLANE, in_plane(1, 1)),
        lax.ppermute(mine[1], PLANE, in_plane(-1, 0)),
    )

    def blocks(after):
        ready = lax.optimization_barrier((*beside, after))
        return call(
            functools.partial(centroid_kernel, scale_root),
            (
                shape((2 * local_count, feat_dim), jnp.bfloat16),
                shape((2 * local_count, 1)),
                shape((owned, feat_dim)),
            ),
            (*mine, *ready[:2]),
            "centroid_blocks",
            4 * local_count * feat_dim,
            share=4,
        )

    scored, orders = [], []

    def scores(order, *parts):
        scored.append(score(parts, cents, bias, scale_root))
        orders.append(order)
        return scored[-1][2]

    def moved(first, second):
        return lax.ppermute(first, "z", along_z(1)), lax.ppermute(second, "z", along_z(-1))

    def both(step):
        return [(NZ - step, 0), (step, 0), (NZ - step, 1), (step, 1)]

    piece = n_rows // 2
    came = [[embeddings, other, up, down, other_core(up), other_core(down)]]
    for _ in range(2):
        up, down = moved(up, down)
        came.append([up, down, other_core(up), other_core(down)])
        if len(came) == 2:
            cents, bias, own_cents = blocks(up)
    up, down = moved(up[:piece], down[piece:])
    done = (
        scores([(0, 0), (0, 1), *both(1)], *came[0]),
        scores(both(2), *came[1]),
        scores(both(3), *came[2]),
    )
    up, down, _ = lax.optimization_barrier((up, down, done))
    scores([(4, 0), (4, 1)], up, down, other_core(jnp.concatenate([up, down])))
    rows, logits, lses = zip(*scored)

    (table,) = call(
        functools.partial(table_kernel, orders), (shape((2 * NZ, LANES)),), lses, "row_table"
    )
    table = joined(table, other_core(table))
    tables = jnp.broadcast_to(table, (NZ, *table.shape))
    table = joined(*lax.all_to_all(tables, "z", 0, 0, tiled=True))

    n_all = 2 * NZ * n_rows
    packed, log_norm = call(
        functools.partial(spread_kernel, orders),
        (
            shape((N_OWNERS, owned * feat_dim // LANES + EXTRA, LANES)),
            shape((1, LANES)),
        ),
        (*logits, *rows, table),
        "spread",
        4 * local_count * n_all * feat_dim,
        2 * local_count * n_all,
    )
    came = lax.all_to_all(packed.astype(jnp.float16), PLANE, 0, 0, tiled=True)
    updated, counts = call(
        update_kernel,
        (shape((owned, feat_dim)), shape((1, owned))),
        (came.astype(jnp.float32), own_cents),
        "update",
    )
    return (updated, counts.reshape(-1), log_norm.reshape(-1))


def solution(mesh):
    split = Mesh(mesh.devices.reshape(2, NZ, 2, 4, 2), AXES)
    block = ("x_lo", "z", "core")
    return jax.shard_map(
        local,
        mesh=split,
        in_specs=(P(AXES, None), P(block, None), P(block)),
        out_specs=(P(AXES, None), P(AXES), P(AXES)),
        check_vma=False,
    )
```

```python
import functools
import math

import jax
import jax.numpy as jnp
from jax import lax
from jax.experimental import pallas as pl
from jax.experimental.pallas import tpu as pltpu
from jax.sharding import Mesh
from jax.sharding import PartitionSpec as P

prior_mass = 1.0

AXES = ("x_lo", "z", "core", "y", "x_hi")
OWNERS = ("x_lo", "y", "x_hi")
NZ, N_OWNERS = 8, 16
LANES = 128
VMEM = pl.BlockSpec(memory_space=pltpu.VMEM)
SHARE = 4
EXTRA = 8


def along_z(step):
    return [(i, (i + step) % NZ) for i in range(NZ)]


def other_core(array):
    return lax.ppermute(array, "core", [(0, 1), (1, 0)])


def call(kernel, outs, args, name, flops=0, transcendentals=0, share=1, vmem=24):
    size = sum(a.size * a.dtype.itemsize for a in (*args, *outs)) // share
    return pl.pallas_call(
        kernel,
        out_shape=outs,
        in_specs=[VMEM] * len(args),
        out_specs=(VMEM,) * len(outs),
        compiler_params=pltpu.CompilerParams(vmem_limit_bytes=vmem * 1024 * 1024),
        cost_estimate=pl.CostEstimate(
            flops=flops // share, bytes_accessed=size, transcendentals=transcendentals // share
        ),
        name=name,
    )(*args)


def shape(dims, dtype=jnp.float32):
    return jax.ShapeDtypeStruct(dims, dtype)


def column(row):
    n = row.shape[1]
    return jnp.concatenate(
        [jnp.broadcast_to(row[:, i : i + LANES], (LANES, LANES)).T[:, :1] for i in range(0, n, LANES)]
    )


def bias_of(cents, weight_row, scale_root):
    wide = cents.astype(jnp.float32)
    half_sq = 0.5 * jnp.sum(wide * wide, axis=1, keepdims=True)
    return column(weight_row) - half_sq * (1.0 / scale_root)


def own_kernel(scale_root, cent_in, weight_ref, rows_in, cent_ref, bias_ref, rows_ref, owned_ref):
    cent_ref[...] = cent_in[...]
    bias_ref[...] = bias_of(cent_in[...], weight_ref[...], scale_root)
    rows_ref[...] = rows_in[...]
    owned = owned_ref.shape[0]
    first = (lax.axis_index("y") * 2 + lax.axis_index("x_hi")) * owned
    owned_ref[...] = cent_in[pl.ds(pl.multiple_of(first, owned), owned), :].astype(jnp.float32)


def other_kernel(scale_root, cent_ref, weight_ref, bias_ref):
    bias_ref[...] = bias_of(cent_ref[...], weight_ref[...], scale_root)


def row_of(step):
    z, core = lax.axis_index("z"), lax.axis_index("core")
    first = lax.rem(z + step, NZ) * 2
    return first + core, first + 1 - core


def score_kernel(scale_root, n_parts, n_blocks, *refs):
    parts, blocks = refs[:n_parts], refs[n_parts : n_parts + 2 * n_blocks]
    rows_ref, lse_ref = refs[n_parts + 2 * n_blocks :][:2]
    logits_refs = refs[n_parts + 2 * n_blocks + 2 :]
    at = 0
    for part in parts:
        rows_ref[at : at + part.shape[0], :] = part[...]
        at += part.shape[0]
    tile = 256
    for k in range(0, at, tile):
        peak, logits = None, []
        for i, logits_ref in enumerate(logits_refs):
            cent_ref, bias_ref = blocks[2 * i : 2 * i + 2]
            dots = lax.dot_general(
                cent_ref[...], rows_ref[k : k + tile, :], (((1,), (1,)), ((), ())),
                preferred_element_type=jnp.float32,
            )
            logits.append(dots * (1.0 / scale_root) + bias_ref[...])
            logits_ref[:, k : k + tile] = logits[-1]
            top = jnp.max(logits[-1], axis=0, keepdims=True)
            peak = top if peak is None else jnp.maximum(peak, top)
        mass = sum(jnp.sum(jnp.exp(l - peak), axis=0, keepdims=True) for l in logits)
        lse = peak + jnp.log(mass)
        for i in range(tile // LANES):
            row = k // LANES + i
            lse_ref[row : row + 1, :] = lse[:, i * LANES : (i + 1) * LANES]


def score(parts, blocks, scale_root):
    count, depth = sum(p.shape[0] for p in parts), parts[0].shape[1]
    n_cent = blocks[0][0].shape[0]
    return call(
        functools.partial(score_kernel, scale_root, len(parts), len(blocks)),
        (
            shape((count, depth), jnp.bfloat16),
            shape((count // LANES, LANES)),
            *[shape((n_cent, count))] * len(blocks),
        ),
        (*parts, *(a for block in blocks for a in block)),
        "score",
        2 * n_cent * count * depth * len(blocks),
        n_cent * count * len(blocks),
        SHARE,
    )


def table_kernel(orders, *refs):
    table_ref = refs[-1]
    seen = set()
    for order, lse in zip(orders, refs[:-1]):
        for i, (dist, side) in enumerate(order):
            here = pl.ds(row_of(dist)[side], 1)
            value = lse[i : i + 1, :]
            table_ref[here, :] = joined(table_ref[here, :], value) if (dist, side) in seen else value
            seen.add((dist, side))


def joined(*tables):
    top = functools.reduce(jnp.maximum, tables)
    return top + jnp.log(sum(jnp.exp(t - top) for t in tables))


def spread_kernel(orders, *refs):
    n = len(orders)
    logits, rows = (refs[:n], refs[n : 2 * n]), refs[2 * n : 3 * n]
    norm_ref, packed_ref, own_ref = refs[3 * n :]
    tile, depth = logits[0][0].shape[0], rows[0].shape[1]
    owned = 2 * tile // N_OWNERS
    x_lo = lax.axis_index("x_lo")
    for block in range(2):
        first = lax.rem(x_lo + block, 2) * (tile // owned)
        total, count = None, None
        for order, logits_ref, rows_ref in zip(orders, logits[block], rows):
            resp = []
            for i, (dist, side) in enumerate(order):
                norm = norm_ref[pl.ds(row_of(dist)[side], 1), :]
                r = jnp.exp(logits_ref[:, i * LANES : (i + 1) * LANES] - norm)
                count = r if count is None else count + r
                resp.append(r.astype(jnp.bfloat16))
            part = jnp.dot(
                jnp.concatenate(resp, axis=1), rows_ref[...], preferred_element_type=jnp.float32
            )
            total = part if total is None else total + part
        count = jnp.sum(count, axis=1, keepdims=True)
        top = jnp.max(jnp.abs(total), axis=1, keepdims=True)
        scale = jnp.maximum(top * 2.0**-14, 2.0**-14).astype(jnp.bfloat16).astype(jnp.float32)
        total = total * (1.0 / scale)
        high = count.astype(jnp.bfloat16).astype(jnp.float32)
        middle = (count - high).astype(jnp.bfloat16).astype(jnp.float32)
        low = count - high - middle
        lane = lax.broadcasted_iota(jnp.int32, (tile, LANES), 1)
        extra = jnp.zeros((tile, LANES), jnp.float32)
        for i, value in enumerate((scale, high, middle * 2.0**8, low * 2.0**16)):
            extra = jnp.where(lane == i, value, extra)
        extra = extra.T[:EXTRA, :]
        at = depth // LANES * owned
        for b in range(tile // owned):
            owner = first + b
            for j in range(depth // LANES):
                packed_ref[owner, j * owned : (j + 1) * owned, :] = total[
                    b * owned : (b + 1) * owned, j * LANES : (j + 1) * LANES
                ]
            packed_ref[owner, at : at + EXTRA, :] = jnp.concatenate(
                [
                    extra[:, b * owned : (b + 1) * owned],
                    jnp.zeros((EXTRA, LANES - owned), jnp.float32),
                ],
                axis=1,
            )
    own_ref[...] = norm_ref[pl.ds(row_of(0)[0], 1), :]


def update_kernel(came_ref, own_ref, updated_ref, counts_ref):
    owned, depth = updated_ref.shape
    at = depth // LANES * owned
    extra = jnp.concatenate([came_ref[i, at : at + EXTRA, :] for i in range(N_OWNERS)])
    counts = None
    for i in range(N_OWNERS):
        e = i * EXTRA
        c = extra[e + 1 : e + 2] + (extra[e + 2 : e + 3] * 2.0**-8 + extra[e + 3 : e + 4] * 2.0**-16)
        counts = c if counts is None else counts + c
    counts_ref[...] = counts[:, :owned]
    turned = extra.T
    mass = jnp.broadcast_to(counts, (LANES, LANES)).T[:owned, :1] + prior_mass
    for j in range(depth // LANES):
        total = None
        for i in range(N_OWNERS):
            scale = turned[:owned, i * EXTRA : i * EXTRA + 1]
            part = came_ref[i, j * owned : (j + 1) * owned, :] * scale
            total = part if total is None else total + part
        here = slice(j * LANES, (j + 1) * LANES)
        updated_ref[:, here] = (total + prior_mass * own_ref[:, here]) / mass


def local(embeddings, centroids, log_weight):
    local_count, feat_dim = centroids.shape
    n_rows = embeddings.shape[0]
    scale_root = math.sqrt(feat_dim)
    owned = local_count // 8

    up = lax.ppermute(embeddings, "z", along_z(1))
    down = lax.ppermute(embeddings, "z", along_z(-1))
    other = other_core(embeddings)
    weight = log_weight[None, :]
    cents_beside = lax.ppermute(centroids, "x_lo", [(0, 1), (1, 0)])
    weight_beside = lax.ppermute(weight, "x_lo", [(0, 1), (1, 0)])
    cents, bias, mine, owned_cents = call(
        functools.partial(own_kernel, scale_root),
        (
            shape(centroids.shape, jnp.bfloat16),
            shape((local_count, 1)),
            shape(embeddings.shape, jnp.bfloat16),
            shape((owned, feat_dim)),
        ),
        (centroids, weight, embeddings),
        "own_block",
        share=SHARE,
    )
    here = cents, bias
    up, down = lax.optimization_barrier((up, down, cents, bias, mine, owned_cents))[:2]
    scored, orders = [], []

    def scores(order, parts, *blocks):
        rows, lse, *logits = score(parts, blocks, scale_root)
        scored.append(lse)
        orders.append(order)
        return rows, lse, logits

    def moved(first, second):
        return lax.ppermute(first, "z", along_z(1)), lax.ppermute(second, "z", along_z(-1))

    def pair(step, side):
        return [(NZ - step, side), (step, side)]

    piece = n_rows // 2
    order1 = [(0, 0), (0, 1), *pair(1, 0)]
    first = [mine, other, up, down]
    side = [other_core(up), other_core(down)]
    up, down = moved(up, down)
    rows1, lse, (near1,) = scores(order1, first, here)
    up, down = lax.optimization_barrier((up, down, lse))[:2]
    order2 = pair(1, 1) + pair(2, 0)
    second = [*side, up, down]
    side = [other_core(up), other_core(down)]
    up, down = moved(up, down)
    rows2, lse, (near2,) = scores(order2, second, here)
    cents_beside, weight_beside = lax.optimization_barrier((cents_beside, weight_beside, up))[:2]
    (bias_beside,) = call(
        functools.partial(other_kernel, scale_root),
        (shape((local_count, 1)),),
        (cents_beside, weight_beside),
        "other_block",
        share=SHARE,
    )
    there = cents_beside, bias_beside
    order3 = pair(2, 1) + pair(3, 0)
    third = [*side, up, down]
    side = [other_core(up), other_core(down)]
    up, down = moved(up[:piece], down[piece:])
    _, lse1, (far1,) = scores(order1, [rows1], there)
    _, lse2, (far2,) = scores(order2, [rows2], there)
    rows3, lse3, (near3, far3) = scores(order3, third, here, there)
    rows4, lse4, (near4, far4) = scores(pair(3, 1), side, here, there)
    up, down = lax.optimization_barrier((up, down, lse1, lse2, lse3, lse4))[:2]
    last = [up, down, other_core(jnp.concatenate([up, down]))]
    rows5, _, (near5, far5) = scores([(4, 0), (4, 1)], last, here, there)
    groups = [
        (order1, rows1, near1, far1),
        (order2, rows2, near2, far2),
        (order3, rows3, near3, far3),
        (pair(3, 1), rows4, near4, far4),
        ([(4, 0), (4, 1)], rows5, near5, far5),
    ]

    (table,) = call(
        functools.partial(table_kernel, orders), (shape((2 * NZ, LANES)),), scored, "row_table"
    )
    table = joined(table, other_core(table))
    tables = jnp.broadcast_to(table, (NZ, *table.shape))
    table = joined(*lax.all_to_all(tables, "z", 0, 0, tiled=True))

    n_all = 2 * NZ * n_rows
    packed, log_norm = call(
        functools.partial(spread_kernel, [o for o, *_ in groups]),
        (
            shape((N_OWNERS, owned * feat_dim // LANES + EXTRA, LANES)),
            shape((1, LANES)),
        ),
        (
            *(group[2] for group in groups),
            *(group[3] for group in groups),
            *(group[1] for group in groups),
            table,
        ),
        "spread",
        4 * local_count * n_all * feat_dim,
        2 * local_count * n_all,
    )
    came = lax.all_to_all(packed.astype(jnp.float16), OWNERS, 0, 0, tiled=True)
    updated, counts = call(
        update_kernel,
        (shape((owned, feat_dim)), shape((1, owned))),
        (came.astype(jnp.float32), owned_cents),
        "update",
    )
    return (updated, counts.reshape(-1), log_norm.reshape(-1))


def solution(mesh):
    split = Mesh(mesh.devices.reshape(2, NZ, 2, 4, 2), AXES)
    block = ("x_lo", "z", "core")
    return jax.shard_map(
        local,
        mesh=split,
        in_specs=(P(AXES, None), P(block, None), P(block)),
        out_specs=(P(AXES, None), P(AXES), P(AXES)),
        check_vma=False,
    )
```

```python
import functools
import math

import jax
import jax.numpy as jnp
from jax import lax
from jax.experimental import pallas as pl
from jax.experimental.pallas import tpu as pltpu
from jax.sharding import Mesh
from jax.sharding import PartitionSpec as P

prior_mass = 1.0

AXES = ("x_lo", "z", "core", "y", "x_hi")
OWNERS = ("x_lo", "y", "x_hi")
NZ, N_OWNERS = 8, 16
LANES = 128
VMEM = pl.BlockSpec(memory_space=pltpu.VMEM)
SHARE = 4
EXTRA = 8


def along_z(step):
    return [(i, (i + step) % NZ) for i in range(NZ)]


def other_core(array):
    return lax.ppermute(array, "core", [(0, 1), (1, 0)])


def call(kernel, outs, args, name, flops=0, transcendentals=0, share=1, vmem=24):
    size = sum(a.size * a.dtype.itemsize for a in (*args, *outs)) // share
    return pl.pallas_call(
        kernel,
        out_shape=outs,
        in_specs=[VMEM] * len(args),
        out_specs=(VMEM,) * len(outs),
        compiler_params=pltpu.CompilerParams(vmem_limit_bytes=vmem * 1024 * 1024),
        cost_estimate=pl.CostEstimate(
            flops=flops // share, bytes_accessed=size, transcendentals=transcendentals // share
        ),
        name=name,
    )(*args)


def shape(dims, dtype=jnp.float32):
    return jax.ShapeDtypeStruct(dims, dtype)


def column(row):
    n = row.shape[1]
    return jnp.concatenate(
        [jnp.broadcast_to(row[:, i : i + LANES], (LANES, LANES)).T[:, :1] for i in range(0, n, LANES)]
    )


def bias_of(cents, weight_row, scale_root):
    wide = cents.astype(jnp.float32)
    half_sq = 0.5 * jnp.sum(wide * wide, axis=1, keepdims=True)
    return column(weight_row) - half_sq * (1.0 / scale_root)


def own_kernel(scale_root, cent_in, weight_ref, rows_in, cent_ref, bias_ref, rows_ref, owned_ref):
    cent_ref[...] = cent_in[...]
    bias_ref[...] = bias_of(cent_in[...], weight_ref[...], scale_root)
    rows_ref[...] = rows_in[...]
    owned = owned_ref.shape[0]
    first = (lax.axis_index("y") * 2 + lax.axis_index("x_hi")) * owned
    owned_ref[...] = cent_in[pl.ds(pl.multiple_of(first, owned), owned), :].astype(jnp.float32)


def other_kernel(scale_root, cent_ref, weight_ref, bias_ref):
    bias_ref[...] = bias_of(cent_ref[...], weight_ref[...], scale_root)


def row_of(step):
    z, core = lax.axis_index("z"), lax.axis_index("core")
    first = lax.rem(z + step, NZ) * 2
    return first + core, first + 1 - core


def score_kernel(scale_root, n_parts, n_blocks, *refs):
    parts, blocks = refs[:n_parts], refs[n_parts : n_parts + 2 * n_blocks]
    lse_ref, *logits_refs = refs[n_parts + 2 * n_blocks :]
    rows_ref, at = parts[0], parts[0].shape[0]
    if n_parts > 1:
        *logits_refs, rows_ref = logits_refs
        at = 0
        for part in parts:
            rows_ref[at : at + part.shape[0], :] = part[...]
            at += part.shape[0]
    tile = 256
    for k in range(0, at, tile):
        peak, logits = None, []
        for i, logits_ref in enumerate(logits_refs):
            cent_ref, bias_ref = blocks[2 * i : 2 * i + 2]
            dots = lax.dot_general(
                cent_ref[...], rows_ref[k : k + tile, :], (((1,), (1,)), ((), ())),
                preferred_element_type=jnp.float32,
            )
            logits.append(dots * (1.0 / scale_root) + bias_ref[...])
            logits_ref[:, k : k + tile] = logits[-1]
            top = jnp.max(logits[-1], axis=0, keepdims=True)
            peak = top if peak is None else jnp.maximum(peak, top)
        mass = sum(jnp.sum(jnp.exp(l - peak), axis=0, keepdims=True) for l in logits)
        lse = peak + jnp.log(mass)
        for i in range(tile // LANES):
            row = k // LANES + i
            lse_ref[row : row + 1, :] = lse[:, i * LANES : (i + 1) * LANES]


def score(parts, blocks, scale_root):
    count, depth = sum(p.shape[0] for p in parts), parts[0].shape[1]
    n_cent = blocks[0][0].shape[0]
    outs = [shape((count // LANES, LANES))] + [shape((n_cent, count))] * len(blocks)
    if len(parts) > 1:
        outs.append(shape((count, depth), jnp.bfloat16))
    found = call(
        functools.partial(score_kernel, scale_root, len(parts), len(blocks)),
        tuple(outs),
        (*parts, *(a for block in blocks for a in block)),
        "score",
        2 * n_cent * count * depth * len(blocks),
        n_cent * count * len(blocks),
        SHARE,
    )
    rows = found[-1] if len(parts) > 1 else parts[0]
    return rows, found[0], found[1 : 1 + len(blocks)]


def table_kernel(orders, *refs):
    table_ref = refs[-1]
    seen = set()
    for order, lse in zip(orders, refs[:-1]):
        for i, (dist, side) in enumerate(order):
            here = pl.ds(row_of(dist)[side], 1)
            value = lse[i : i + 1, :]
            table_ref[here, :] = joined(table_ref[here, :], value) if (dist, side) in seen else value
            seen.add((dist, side))


def joined(*tables):
    top = functools.reduce(jnp.maximum, tables)
    return top + jnp.log(sum(jnp.exp(t - top) for t in tables))


def spread_kernel(orders, *refs):
    n = len(orders)
    logits, rows = (refs[:n], refs[n : 2 * n]), refs[2 * n : 3 * n]
    norm_ref, packed_ref, own_ref = refs[3 * n :]
    tile, depth = logits[0][0].shape[0], rows[0].shape[1]
    owned = 2 * tile // N_OWNERS
    x_lo = lax.axis_index("x_lo")
    for block in range(2):
        first = lax.rem(x_lo + block, 2) * (tile // owned)
        total, count = None, None
        for order, logits_ref, rows_ref in zip(orders, logits[block], rows):
            resp = []
            for i, (dist, side) in enumerate(order):
                norm = norm_ref[pl.ds(row_of(dist)[side], 1), :]
                r = jnp.exp(logits_ref[:, i * LANES : (i + 1) * LANES] - norm)
                count = r if count is None else count + r
                resp.append(r.astype(jnp.bfloat16))
            part = jnp.dot(
                jnp.concatenate(resp, axis=1), rows_ref[...], preferred_element_type=jnp.float32
            )
            total = part if total is None else total + part
        count = jnp.sum(count, axis=1, keepdims=True)
        top = jnp.max(jnp.abs(total), axis=1, keepdims=True)
        scale = jnp.maximum(top * 2.0**-14, 2.0**-14).astype(jnp.bfloat16).astype(jnp.float32)
        total = total * (1.0 / scale)
        high = count.astype(jnp.bfloat16).astype(jnp.float32)
        middle = (count - high).astype(jnp.bfloat16).astype(jnp.float32)
        low = count - high - middle
        lane = lax.broadcasted_iota(jnp.int32, (tile, LANES), 1)
        extra = jnp.zeros((tile, LANES), jnp.float32)
        for i, value in enumerate((scale, high, middle * 2.0**8, low * 2.0**16)):
            extra = jnp.where(lane == i, value, extra)
        extra = extra.T[:EXTRA, :]
        at = depth // LANES * owned
        for b in range(tile // owned):
            owner = first + b
            for j in range(depth // LANES):
                packed_ref[owner, j * owned : (j + 1) * owned, :] = total[
                    b * owned : (b + 1) * owned, j * LANES : (j + 1) * LANES
                ]
            packed_ref[owner, at : at + EXTRA, :] = jnp.concatenate(
                [
                    extra[:, b * owned : (b + 1) * owned],
                    jnp.zeros((EXTRA, LANES - owned), jnp.float32),
                ],
                axis=1,
            )
    own_ref[...] = norm_ref[pl.ds(row_of(0)[0], 1), :]


def update_kernel(came_ref, own_ref, updated_ref, counts_ref):
    owned, depth = updated_ref.shape
    at = depth // LANES * owned
    extra = jnp.concatenate([came_ref[i, at : at + EXTRA, :] for i in range(N_OWNERS)])
    counts = None
    for i in range(N_OWNERS):
        e = i * EXTRA
        c = extra[e + 1 : e + 2] + (extra[e + 2 : e + 3] * 2.0**-8 + extra[e + 3 : e + 4] * 2.0**-16)
        counts = c if counts is None else counts + c
    counts_ref[...] = counts[:, :owned]
    turned = extra.T
    mass = jnp.broadcast_to(counts, (LANES, LANES)).T[:owned, :1] + prior_mass
    for j in range(depth // LANES):
        total = None
        for i in range(N_OWNERS):
            scale = turned[:owned, i * EXTRA : i * EXTRA + 1]
            part = came_ref[i, j * owned : (j + 1) * owned, :] * scale
            total = part if total is None else total + part
        here = slice(j * LANES, (j + 1) * LANES)
        updated_ref[:, here] = (total + prior_mass * own_ref[:, here]) / mass


def local(embeddings, centroids, log_weight):
    local_count, feat_dim = centroids.shape
    n_rows = embeddings.shape[0]
    scale_root = math.sqrt(feat_dim)
    owned = local_count // 8

    up = lax.ppermute(embeddings, "z", along_z(1))
    down = lax.ppermute(embeddings, "z", along_z(-1))
    other = other_core(embeddings)
    weight = log_weight[None, :]
    cents_beside = lax.ppermute(centroids, "x_lo", [(0, 1), (1, 0)])
    weight_beside = lax.ppermute(weight, "x_lo", [(0, 1), (1, 0)])
    cents, bias, mine, owned_cents = call(
        functools.partial(own_kernel, scale_root),
        (
            shape(centroids.shape, jnp.bfloat16),
            shape((local_count, 1)),
            shape(embeddings.shape, jnp.bfloat16),
            shape((owned, feat_dim)),
        ),
        (centroids, weight, embeddings),
        "own_block",
        share=SHARE,
    )
    here = cents, bias
    up, down = lax.optimization_barrier((up, down, cents, bias, mine, owned_cents))[:2]
    scored, orders = [], []

    def scores(order, parts, *blocks):
        rows, lse, logits = score(parts, blocks, scale_root)
        scored.append(lse)
        orders.append(order)
        return rows, lse, logits

    def moved(first, second):
        return lax.ppermute(first, "z", along_z(1)), lax.ppermute(second, "z", along_z(-1))

    def pair(step, side):
        return [(NZ - step, side), (step, side)]

    piece = n_rows // 2
    order1 = [(0, 0), (0, 1), *pair(1, 0)]
    first = [mine, other, up, down]
    side = [other_core(up), other_core(down)]
    up, down = moved(up, down)
    rows1, lse, (near1,) = scores(order1, first, here)
    up, down = lax.optimization_barrier((up, down, lse))[:2]
    order2 = pair(1, 1) + pair(2, 0)
    second = [*side, up, down]
    side = [other_core(up), other_core(down)]
    up, down = moved(up, down)
    rows2, lse, (near2,) = scores(order2, second, here)
    cents_beside, weight_beside = lax.optimization_barrier((cents_beside, weight_beside, up))[:2]
    (bias_beside,) = call(
        functools.partial(other_kernel, scale_root),
        (shape((local_count, 1)),),
        (cents_beside, weight_beside),
        "other_block",
        share=SHARE,
    )
    there = cents_beside, bias_beside
    order3 = pair(2, 1) + pair(3, 0)
    third = [*side, up, down]
    side = [other_core(up), other_core(down)]
    up, down = moved(up[:piece], down[piece:])
    _, lse1, (far1,) = scores(order1, [rows1], there)
    _, lse2, (far2,) = scores(order2, [rows2], there)
    rows3, lse3, (near3, far3) = scores(order3, third, here, there)
    rows4, lse4, (near4, far4) = scores(pair(3, 1), side, here, there)
    up, down = lax.optimization_barrier((up, down, lse1, lse2, lse3, lse4))[:2]
    last = [up, down, other_core(jnp.concatenate([up, down]))]
    rows5, _, (near5, far5) = scores([(4, 0), (4, 1)], last, here, there)
    groups = [
        (order1, rows1, near1, far1),
        (order2, rows2, near2, far2),
        (order3, rows3, near3, far3),
        (pair(3, 1), rows4, near4, far4),
        ([(4, 0), (4, 1)], rows5, near5, far5),
    ]

    (table,) = call(
        functools.partial(table_kernel, orders), (shape((2 * NZ, LANES)),), scored, "row_table"
    )
    table = joined(table, other_core(table))
    tables = jnp.broadcast_to(table, (NZ, *table.shape))
    table = joined(*lax.all_to_all(tables, "z", 0, 0, tiled=True))

    n_all = 2 * NZ * n_rows
    packed, log_norm = call(
        functools.partial(spread_kernel, [o for o, *_ in groups]),
        (
            shape((N_OWNERS, owned * feat_dim // LANES + EXTRA, LANES)),
            shape((1, LANES)),
        ),
        (
            *(group[2] for group in groups),
            *(group[3] for group in groups),
            *(group[1] for group in groups),
            table,
        ),
        "spread",
        4 * local_count * n_all * feat_dim,
        2 * local_count * n_all,
    )
    came = lax.all_to_all(packed.astype(jnp.float16), OWNERS, 0, 0, tiled=True)
    updated, counts = call(
        update_kernel,
        (shape((owned, feat_dim)), shape((1, owned))),
        (came.astype(jnp.float32), owned_cents),
        "update",
    )
    return (updated, counts.reshape(-1), log_norm.reshape(-1))


def solution(mesh):
    split = Mesh(mesh.devices.reshape(2, NZ, 2, 4, 2), AXES)
    block = ("x_lo", "z", "core")
    return jax.shard_map(
        local,
        mesh=split,
        in_specs=(P(AXES, None), P(block, None), P(block)),
        out_specs=(P(AXES, None), P(AXES), P(AXES)),
        check_vma=False,
    )
```

```python
import functools
import math

import jax
import jax.numpy as jnp
from jax import lax
from jax.experimental import pallas as pl
from jax.experimental.pallas import tpu as pltpu
from jax.sharding import Mesh
from jax.sharding import PartitionSpec as P

prior_mass = 1.0

AXES = ("x_lo", "z", "core", "y", "x_hi")
OWNERS = ("x_lo", "y", "x_hi")
NZ, N_OWNERS = 8, 16
LANES = 128
VMEM = pl.BlockSpec(memory_space=pltpu.VMEM)
SHARE = 4
EXTRA = 8


def along_z(step):
    return [(i, (i + step) % NZ) for i in range(NZ)]


def other_core(array):
    return lax.ppermute(array, "core", [(0, 1), (1, 0)])


def call(kernel, outs, args, name, flops=0, transcendentals=0, share=1, vmem=24):
    size = sum(a.size * a.dtype.itemsize for a in (*args, *outs)) // share
    return pl.pallas_call(
        kernel,
        out_shape=outs,
        in_specs=[VMEM] * len(args),
        out_specs=(VMEM,) * len(outs),
        compiler_params=pltpu.CompilerParams(vmem_limit_bytes=vmem * 1024 * 1024),
        cost_estimate=pl.CostEstimate(
            flops=flops // share, bytes_accessed=size, transcendentals=transcendentals // share
        ),
        name=name,
    )(*args)


def shape(dims, dtype=jnp.float32):
    return jax.ShapeDtypeStruct(dims, dtype)


def column(row):
    n = row.shape[1]
    return jnp.concatenate(
        [jnp.broadcast_to(row[:, i : i + LANES], (LANES, LANES)).T[:, :1] for i in range(0, n, LANES)]
    )


def bias_of(cents, weight_row, scale_root):
    wide = cents.astype(jnp.float32)
    half_sq = 0.5 * jnp.sum(wide * wide, axis=1, keepdims=True)
    return column(weight_row) - half_sq * (1.0 / scale_root)


def own_kernel(scale_root, cent_in, weight_ref, rows_in, cent_ref, bias_ref, rows_ref, owned_ref):
    cent_ref[...] = cent_in[...]
    bias_ref[...] = bias_of(cent_in[...], weight_ref[...], scale_root)
    rows_ref[...] = rows_in[...]
    owned = owned_ref.shape[0]
    first = (lax.axis_index("y") * 2 + lax.axis_index("x_hi")) * owned
    owned_ref[...] = cent_in[pl.ds(pl.multiple_of(first, owned), owned), :].astype(jnp.float32)


def other_kernel(scale_root, cent_ref, weight_ref, bias_ref):
    bias_ref[...] = bias_of(cent_ref[...], weight_ref[...], scale_root)


def row_of(step):
    z, core = lax.axis_index("z"), lax.axis_index("core")
    first = lax.rem(z + step, NZ) * 2
    return first + core, first + 1 - core


def score_kernel(scale_root, n_parts, n_blocks, *refs):
    parts, blocks = refs[:n_parts], refs[n_parts : n_parts + 2 * n_blocks]
    lse_ref, *logits_refs = refs[n_parts + 2 * n_blocks :]
    rows_ref, at = parts[0], parts[0].shape[0]
    if n_parts > 1:
        *logits_refs, rows_ref = logits_refs
        at = 0
        for part in parts:
            rows_ref[at : at + part.shape[0], :] = part[...]
            at += part.shape[0]
    tile = 256
    for k in range(0, at, tile):
        peak, logits = None, []
        for i, logits_ref in enumerate(logits_refs):
            cent_ref, bias_ref = blocks[2 * i : 2 * i + 2]
            dots = lax.dot_general(
                cent_ref[...], rows_ref[k : k + tile, :], (((1,), (1,)), ((), ())),
                preferred_element_type=jnp.float32,
            )
            logits.append(dots * (1.0 / scale_root) + bias_ref[...])
            logits_ref[:, k : k + tile] = logits[-1]
            top = jnp.max(logits[-1], axis=0, keepdims=True)
            peak = top if peak is None else jnp.maximum(peak, top)
        mass = sum(jnp.sum(jnp.exp(l - peak), axis=0, keepdims=True) for l in logits)
        lse = peak + jnp.log(mass)
        for i in range(tile // LANES):
            row = k // LANES + i
            lse_ref[row : row + 1, :] = lse[:, i * LANES : (i + 1) * LANES]


def score(parts, blocks, scale_root):
    count, depth = sum(p.shape[0] for p in parts), parts[0].shape[1]
    n_cent = blocks[0][0].shape[0]
    outs = [shape((count // LANES, LANES))] + [shape((n_cent, count))] * len(blocks)
    if len(parts) > 1:
        outs.append(shape((count, depth), jnp.bfloat16))
    found = call(
        functools.partial(score_kernel, scale_root, len(parts), len(blocks)),
        tuple(outs),
        (*parts, *(a for block in blocks for a in block)),
        "score",
        2 * n_cent * count * depth * len(blocks),
        n_cent * count * len(blocks),
        SHARE,
    )
    rows = found[-1] if len(parts) > 1 else parts[0]
    return rows, found[0], found[1 : 1 + len(blocks)]


def table_kernel(orders, *refs):
    table_ref = refs[-1]
    seen = set()
    for order, lse in zip(orders, refs[:-1]):
        for i, (dist, side) in enumerate(order):
            here = pl.ds(row_of(dist)[side], 1)
            value = lse[i : i + 1, :]
            table_ref[here, :] = joined(table_ref[here, :], value) if (dist, side) in seen else value
            seen.add((dist, side))


def joined(*tables):
    top = functools.reduce(jnp.maximum, tables)
    return top + jnp.log(sum(jnp.exp(t - top) for t in tables))


def spread_kernel(orders, *refs):
    n = len(orders)
    logits, rows = (refs[:n], refs[n : 2 * n]), refs[2 * n : 3 * n]
    norm_ref, packed_ref, own_ref = refs[3 * n :]
    tile, depth = logits[0][0].shape[0], rows[0].shape[1]
    owned = 2 * tile // N_OWNERS
    x_lo = lax.axis_index("x_lo")
    part_tile = tile // 2
    for block, k in ((0, 0), (0, part_tile), (1, 0), (1, part_tile)):
        first = lax.rem(x_lo + block, 2) * (tile // owned) + k // owned
        total, count = None, None
        for order, logits_ref, rows_ref in zip(orders, logits[block], rows):
            resp = []
            for i, (dist, side) in enumerate(order):
                norm = norm_ref[pl.ds(row_of(dist)[side], 1), :]
                r = jnp.exp(logits_ref[k : k + part_tile, i * LANES : (i + 1) * LANES] - norm)
                count = r if count is None else count + r
                resp.append(r.astype(jnp.bfloat16))
            part = jnp.dot(
                jnp.concatenate(resp, axis=1), rows_ref[...], preferred_element_type=jnp.float32
            )
            total = part if total is None else total + part
        count = jnp.sum(count, axis=1, keepdims=True)
        top = jnp.max(jnp.abs(total), axis=1, keepdims=True)
        scale = jnp.maximum(top * 2.0**-14, 2.0**-14).astype(jnp.bfloat16).astype(jnp.float32)
        total = total * (1.0 / scale)
        high = count.astype(jnp.bfloat16).astype(jnp.float32)
        middle = (count - high).astype(jnp.bfloat16).astype(jnp.float32)
        low = count - high - middle
        lane = lax.broadcasted_iota(jnp.int32, (part_tile, LANES), 1)
        extra = jnp.zeros((part_tile, LANES), jnp.float32)
        for i, value in enumerate((scale, high, middle * 2.0**8, low * 2.0**16)):
            extra = jnp.where(lane == i, value, extra)
        extra = extra.T[:EXTRA, :]
        at = depth // LANES * owned
        for b in range(part_tile // owned):
            owner = first + b
            for j in range(depth // LANES):
                packed_ref[owner, j * owned : (j + 1) * owned, :] = total[
                    b * owned : (b + 1) * owned, j * LANES : (j + 1) * LANES
                ]
            packed_ref[owner, at : at + EXTRA, :] = jnp.concatenate(
                [
                    extra[:, b * owned : (b + 1) * owned],
                    jnp.zeros((EXTRA, LANES - owned), jnp.float32),
                ],
                axis=1,
            )
    own_ref[...] = norm_ref[pl.ds(row_of(0)[0], 1), :]


def update_kernel(came_ref, own_ref, updated_ref, counts_ref):
    owned, depth = updated_ref.shape
    at = depth // LANES * owned
    extra = jnp.concatenate([came_ref[i, at : at + EXTRA, :] for i in range(N_OWNERS)])
    counts = None
    for i in range(N_OWNERS):
        e = i * EXTRA
        c = extra[e + 1 : e + 2] + (extra[e + 2 : e + 3] * 2.0**-8 + extra[e + 3 : e + 4] * 2.0**-16)
        counts = c if counts is None else counts + c
    counts_ref[...] = counts[:, :owned]
    turned = extra.T
    mass = jnp.broadcast_to(counts, (LANES, LANES)).T[:owned, :1] + prior_mass
    for j in range(depth // LANES):
        total = None
        for i in range(N_OWNERS):
            scale = turned[:owned, i * EXTRA : i * EXTRA + 1]
            part = came_ref[i, j * owned : (j + 1) * owned, :] * scale
            total = part if total is None else total + part
        here = slice(j * LANES, (j + 1) * LANES)
        updated_ref[:, here] = (total + prior_mass * own_ref[:, here]) / mass


def local(embeddings, centroids, log_weight):
    local_count, feat_dim = centroids.shape
    n_rows = embeddings.shape[0]
    scale_root = math.sqrt(feat_dim)
    owned = local_count // 8

    up = lax.ppermute(embeddings, "z", along_z(1))
    down = lax.ppermute(embeddings, "z", along_z(-1))
    other = other_core(embeddings)
    weight = log_weight[None, :]
    cents_beside = lax.ppermute(centroids, "x_lo", [(0, 1), (1, 0)])
    weight_beside = lax.ppermute(weight, "x_lo", [(0, 1), (1, 0)])
    cents, bias, mine, owned_cents = call(
        functools.partial(own_kernel, scale_root),
        (
            shape(centroids.shape, jnp.bfloat16),
            shape((local_count, 1)),
            shape(embeddings.shape, jnp.bfloat16),
            shape((owned, feat_dim)),
        ),
        (centroids, weight, embeddings),
        "own_block",
        share=SHARE,
    )
    here = cents, bias
    up, down = lax.optimization_barrier((up, down, cents, bias, mine, owned_cents))[:2]
    scored, orders = [], []

    def scores(order, parts, *blocks):
        rows, lse, logits = score(parts, blocks, scale_root)
        scored.append(lse)
        orders.append(order)
        return rows, lse, logits

    def moved(first, second):
        return lax.ppermute(first, "z", along_z(1)), lax.ppermute(second, "z", along_z(-1))

    def pair(step, side):
        return [(NZ - step, side), (step, side)]

    piece = n_rows // 2
    order1 = [(0, 0), (0, 1), *pair(1, 0)]
    first = [mine, other, up, down]
    side = [other_core(up), other_core(down)]
    up, down = moved(up, down)
    rows1, lse, (near1,) = scores(order1, first, here)
    up, down = lax.optimization_barrier((up, down, lse))[:2]
    order2 = pair(1, 1) + pair(2, 0)
    second = [*side, up, down]
    side = [other_core(up), other_core(down)]
    up, down = moved(up, down)
    rows2, lse, (near2,) = scores(order2, second, here)
    cents_beside, weight_beside = lax.optimization_barrier((cents_beside, weight_beside, up, down))[:2]
    (bias_beside,) = call(
        functools.partial(other_kernel, scale_root),
        (shape((local_count, 1)),),
        (cents_beside, weight_beside),
        "other_block",
        share=SHARE,
    )
    there = cents_beside, bias_beside
    order3 = pair(2, 1) + pair(3, 0)
    third = [*side, up, down]
    side = [other_core(up), other_core(down)]
    up, down = moved(up[:piece], down[piece:])
    _, lse1, (far1,) = scores(order1, [rows1], there)
    _, lse2, (far2,) = scores(order2, [rows2], there)
    rows3, lse3, (near3, far3) = scores(order3, third, here, there)
    rows4, lse4, (near4, far4) = scores(pair(3, 1), side, here, there)
    up, down = lax.optimization_barrier((up, down, lse1, lse2, lse3, lse4))[:2]
    last = [up, down, other_core(up), other_core(down)]
    rows5, _, (near5, far5) = scores([(4, 0), (4, 1)], last, here, there)
    groups = [
        (order1, rows1, near1, far1),
        (order2, rows2, near2, far2),
        (order3, rows3, near3, far3),
        (pair(3, 1), rows4, near4, far4),
        ([(4, 0), (4, 1)], rows5, near5, far5),
    ]

    (table,) = call(
        functools.partial(table_kernel, orders), (shape((2 * NZ, LANES)),), scored, "row_table"
    )
    table = joined(table, other_core(table))
    tables = jnp.broadcast_to(table, (NZ, *table.shape))
    table = joined(*lax.all_to_all(tables, "z", 0, 0, tiled=True))

    n_all = 2 * NZ * n_rows
    packed, log_norm = call(
        functools.partial(spread_kernel, [o for o, *_ in groups]),
        (
            shape((N_OWNERS, owned * feat_dim // LANES + EXTRA, LANES)),
            shape((1, LANES)),
        ),
        (
            *(group[2] for group in groups),
            *(group[3] for group in groups),
            *(group[1] for group in groups),
            table,
        ),
        "spread",
        4 * local_count * n_all * feat_dim,
        2 * local_count * n_all,
    )
    came = lax.all_to_all(packed.astype(jnp.float16), OWNERS, 0, 0, tiled=True)
    updated, counts = call(
        update_kernel,
        (shape((owned, feat_dim)), shape((1, owned))),
        (came.astype(jnp.float32), owned_cents),
        "update",
    )
    return (updated, counts.reshape(-1), log_norm.reshape(-1))


def solution(mesh):
    split = Mesh(mesh.devices.reshape(2, NZ, 2, 4, 2), AXES)
    block = ("x_lo", "z", "core")
    return jax.shard_map(
        local,
        mesh=split,
        in_specs=(P(AXES, None), P(block, None), P(block)),
        out_specs=(P(AXES, None), P(AXES), P(AXES)),
        check_vma=False,
    )
```

```python
import functools
import math

import jax
import jax.numpy as jnp
from jax import lax
from jax.experimental import pallas as pl
from jax.experimental.pallas import tpu as pltpu
from jax.sharding import Mesh
from jax.sharding import PartitionSpec as P

prior_mass = 1.0

AXES = ("x_lo", "z", "core", "y", "x_hi")
OWNERS = ("x_lo", "y", "x_hi")
NZ, N_OWNERS = 8, 16
LANES = 128
VMEM = pl.BlockSpec(memory_space=pltpu.VMEM)
SHARE = 4
EXTRA = 8


def along_z(step):
    return [(i, (i + step) % NZ) for i in range(NZ)]


def other_core(array):
    return lax.ppermute(array, "core", [(0, 1), (1, 0)])


def call(kernel, outs, args, name, flops=0, transcendentals=0, share=1, vmem=24):
    size = sum(a.size * a.dtype.itemsize for a in (*args, *outs)) // share
    return pl.pallas_call(
        kernel,
        out_shape=outs,
        in_specs=[VMEM] * len(args),
        out_specs=(VMEM,) * len(outs),
        compiler_params=pltpu.CompilerParams(vmem_limit_bytes=vmem * 1024 * 1024),
        cost_estimate=pl.CostEstimate(
            flops=flops // share, bytes_accessed=size, transcendentals=transcendentals // share
        ),
        name=name,
    )(*args)


def shape(dims, dtype=jnp.float32):
    return jax.ShapeDtypeStruct(dims, dtype)


def column(row):
    n = row.shape[1]
    return jnp.concatenate(
        [jnp.broadcast_to(row[:, i : i + LANES], (LANES, LANES)).T[:, :1] for i in range(0, n, LANES)]
    )


def bias_of(cents, weight_row, scale_root):
    wide = cents.astype(jnp.float32)
    half_sq = 0.5 * jnp.sum(wide * wide, axis=1, keepdims=True)
    return column(weight_row) - half_sq * (1.0 / scale_root)


def own_kernel(scale_root, cent_in, weight_ref, rows_in, cent_ref, bias_ref, rows_ref, owned_ref):
    cent_ref[...] = cent_in[...]
    bias_ref[...] = bias_of(cent_in[...], weight_ref[...], scale_root)
    rows_ref[...] = rows_in[...]
    owned = owned_ref.shape[0]
    first = (lax.axis_index("y") * 2 + lax.axis_index("x_hi")) * owned
    owned_ref[...] = cent_in[pl.ds(pl.multiple_of(first, owned), owned), :].astype(jnp.float32)


def other_kernel(scale_root, cent_ref, weight_ref, bias_ref):
    bias_ref[...] = bias_of(cent_ref[...], weight_ref[...], scale_root)


def row_of(step):
    z, core = lax.axis_index("z"), lax.axis_index("core")
    first = lax.rem(z + step, NZ) * 2
    return first + core, first + 1 - core


def score_kernel(scale_root, n_parts, n_blocks, *refs):
    parts, blocks = refs[:n_parts], refs[n_parts : n_parts + 2 * n_blocks]
    lse_ref, *logits_refs = refs[n_parts + 2 * n_blocks :]
    rows_ref, at = parts[0], parts[0].shape[0]
    if n_parts > 1:
        *logits_refs, rows_ref = logits_refs
        at = 0
        for part in parts:
            rows_ref[at : at + part.shape[0], :] = part[...]
            at += part.shape[0]
    tile = min(256, at)
    for k in range(0, at, tile):
        peak, logits = None, []
        for i, logits_ref in enumerate(logits_refs):
            cent_ref, bias_ref = blocks[2 * i : 2 * i + 2]
            dots = lax.dot_general(
                cent_ref[...], rows_ref[k : k + tile, :], (((1,), (1,)), ((), ())),
                preferred_element_type=jnp.float32,
            )
            logits.append(dots * (1.0 / scale_root) + bias_ref[...])
            logits_ref[:, k : k + tile] = logits[-1]
            top = jnp.max(logits[-1], axis=0, keepdims=True)
            peak = top if peak is None else jnp.maximum(peak, top)
        mass = sum(jnp.sum(jnp.exp(l - peak), axis=0, keepdims=True) for l in logits)
        lse = peak + jnp.log(mass)
        for i in range(tile // LANES):
            row = k // LANES + i
            lse_ref[row : row + 1, :] = lse[:, i * LANES : (i + 1) * LANES]


def score(parts, blocks, scale_root):
    count, depth = sum(p.shape[0] for p in parts), parts[0].shape[1]
    n_cent = blocks[0][0].shape[0]
    outs = [shape((count // LANES, LANES))] + [shape((n_cent, count))] * len(blocks)
    if len(parts) > 1:
        outs.append(shape((count, depth), jnp.bfloat16))
    found = call(
        functools.partial(score_kernel, scale_root, len(parts), len(blocks)),
        tuple(outs),
        (*parts, *(a for block in blocks for a in block)),
        "score",
        2 * n_cent * count * depth * len(blocks),
        n_cent * count * len(blocks),
        SHARE,
    )
    rows = found[-1] if len(parts) > 1 else parts[0]
    return rows, found[0], found[1 : 1 + len(blocks)]


def table_kernel(orders, *refs):
    table_ref = refs[-1]
    seen = set()
    for order, lse in zip(orders, refs[:-1]):
        for i, (dist, side) in enumerate(order):
            here = pl.ds(row_of(dist)[side], 1)
            value = lse[i : i + 1, :]
            table_ref[here, :] = joined(table_ref[here, :], value) if (dist, side) in seen else value
            seen.add((dist, side))


def joined(*tables):
    top = functools.reduce(jnp.maximum, tables)
    return top + jnp.log(sum(jnp.exp(t - top) for t in tables))


def spread_kernel(orders, *refs):
    n = len(orders)
    logits, rows = (refs[:n], refs[n : 2 * n]), refs[2 * n : 3 * n]
    norm_ref, packed_ref, own_ref = refs[3 * n :]
    tile, depth = logits[0][0].shape[0], rows[0].shape[1]
    owned = 2 * tile // N_OWNERS
    x_lo = lax.axis_index("x_lo")
    for block in range(2):
        first = lax.rem(x_lo + block, 2) * (tile // owned)
        total, count = None, None
        for order, logits_ref, rows_ref in zip(orders, logits[block], rows):
            resp = []
            for i, (dist, side) in enumerate(order):
                norm = norm_ref[pl.ds(row_of(dist)[side], 1), :]
                r = jnp.exp(logits_ref[:, i * LANES : (i + 1) * LANES] - norm)
                count = r if count is None else count + r
                resp.append(r.astype(jnp.bfloat16))
            part = jnp.dot(
                jnp.concatenate(resp, axis=1), rows_ref[...], preferred_element_type=jnp.float32
            )
            total = part if total is None else total + part
        count = jnp.sum(count, axis=1, keepdims=True)
        top = jnp.max(jnp.abs(total), axis=1, keepdims=True)
        scale = jnp.maximum(top * 2.0**-14, 2.0**-14).astype(jnp.bfloat16).astype(jnp.float32)
        total = total * (1.0 / scale)
        high = count.astype(jnp.bfloat16).astype(jnp.float32)
        middle = (count - high).astype(jnp.bfloat16).astype(jnp.float32)
        low = count - high - middle
        lane = lax.broadcasted_iota(jnp.int32, (tile, LANES), 1)
        extra = jnp.zeros((tile, LANES), jnp.float32)
        for i, value in enumerate((scale, high, middle * 2.0**8, low * 2.0**16)):
            extra = jnp.where(lane == i, value, extra)
        extra = extra.T[:EXTRA, :]
        at = depth // LANES * owned
        for b in range(tile // owned):
            owner = first + b
            for j in range(depth // LANES):
                packed_ref[owner, j * owned : (j + 1) * owned, :] = total[
                    b * owned : (b + 1) * owned, j * LANES : (j + 1) * LANES
                ]
            packed_ref[owner, at : at + EXTRA, :] = jnp.concatenate(
                [
                    extra[:, b * owned : (b + 1) * owned],
                    jnp.zeros((EXTRA, LANES - owned), jnp.float32),
                ],
                axis=1,
            )
    own_ref[...] = norm_ref[pl.ds(row_of(0)[0], 1), :]


def update_kernel(came_ref, own_ref, updated_ref, counts_ref):
    owned, depth = updated_ref.shape
    at = depth // LANES * owned
    extra = jnp.concatenate([came_ref[i, at : at + EXTRA, :] for i in range(N_OWNERS)])
    counts = None
    for i in range(N_OWNERS):
        e = i * EXTRA
        c = extra[e + 1 : e + 2] + (extra[e + 2 : e + 3] * 2.0**-8 + extra[e + 3 : e + 4] * 2.0**-16)
        counts = c if counts is None else counts + c
    counts_ref[...] = counts[:, :owned]
    turned = extra.T
    mass = jnp.broadcast_to(counts, (LANES, LANES)).T[:owned, :1] + prior_mass
    for j in range(depth // LANES):
        total = None
        for i in range(N_OWNERS):
            scale = turned[:owned, i * EXTRA : i * EXTRA + 1]
            part = came_ref[i, j * owned : (j + 1) * owned, :] * scale
            total = part if total is None else total + part
        here = slice(j * LANES, (j + 1) * LANES)
        updated_ref[:, here] = (total + prior_mass * own_ref[:, here]) / mass


def local(embeddings, centroids, log_weight):
    local_count, feat_dim = centroids.shape
    n_rows = embeddings.shape[0]
    scale_root = math.sqrt(feat_dim)
    owned = local_count // 8

    up = lax.ppermute(embeddings, "z", along_z(1))
    down = lax.ppermute(embeddings, "z", along_z(-1))
    other = other_core(embeddings)
    weight = log_weight[None, :]
    cents_beside = lax.ppermute(centroids, "x_lo", [(0, 1), (1, 0)])
    weight_beside = lax.ppermute(weight, "x_lo", [(0, 1), (1, 0)])
    cents, bias, mine, owned_cents = call(
        functools.partial(own_kernel, scale_root),
        (
            shape(centroids.shape, jnp.bfloat16),
            shape((local_count, 1)),
            shape(embeddings.shape, jnp.bfloat16),
            shape((owned, feat_dim)),
        ),
        (centroids, weight, embeddings),
        "own_block",
        share=SHARE,
    )
    here = cents, bias
    up, down = lax.optimization_barrier((up, down, cents, bias, mine, owned_cents))[:2]
    scored, orders = [], []

    def scores(order, parts, *blocks):
        rows, lse, logits = score(parts, blocks, scale_root)
        scored.append(lse)
        orders.append(order)
        return rows, lse, logits

    def moved(first, second):
        return lax.ppermute(first, "z", along_z(1)), lax.ppermute(second, "z", along_z(-1))

    def pair(step, side):
        return [(NZ - step, side), (step, side)]

    piece = n_rows // 2
    order1 = [(0, 0), (0, 1), *pair(1, 0)]
    first = [mine, other, up, down]
    side = [other_core(up), other_core(down)]
    up, down = moved(up, down)
    rows1, lse, (near1,) = scores(order1, first, here)
    up, down = lax.optimization_barrier((up, down, lse))[:2]
    order2 = pair(1, 1) + pair(2, 0)
    second = [*side, up, down]
    side = [other_core(up), other_core(down)]
    up, down = moved(up, down)
    rows2, lse, (near2,) = scores(order2, second, here)
    cents_beside, weight_beside = lax.optimization_barrier((cents_beside, weight_beside, up))[:2]
    (bias_beside,) = call(
        functools.partial(other_kernel, scale_root),
        (shape((local_count, 1)),),
        (cents_beside, weight_beside),
        "other_block",
        share=SHARE,
    )
    there = cents_beside, bias_beside
    order3 = pair(2, 1) + pair(3, 0)
    third = [*side, up, down]
    side = [other_core(up), other_core(down)]
    up, down = moved(up[:piece], down[piece:])
    _, lse1, (far1,) = scores(order1, [rows1], there)
    _, lse2, (far2,) = scores(order2, [rows2], there)
    rows3, lse3, (near3, far3) = scores(order3, third, here, there)
    rows4, lse4, (near4, far4) = scores(pair(3, 1), side, here, there)
    up, down = lax.optimization_barrier((up, down, lse1, lse2, lse3, lse4))[:2]
    beside = [other_core(up), other_core(down)]
    rows5, _, (near5, far5) = scores([(4, 0)], [up, down], here, there)
    rows6, _, (near6, far6) = scores([(4, 1)], beside, here, there)
    groups = [
        (order1, rows1, near1, far1),
        (order2, rows2, near2, far2),
        (order3, rows3, near3, far3),
        (pair(3, 1), rows4, near4, far4),
        ([(4, 0)], rows5, near5, far5),
        ([(4, 1)], rows6, near6, far6),
    ]

    (table,) = call(
        functools.partial(table_kernel, orders), (shape((2 * NZ, LANES)),), scored, "row_table"
    )
    table = joined(table, other_core(table))
    tables = jnp.broadcast_to(table, (NZ, *table.shape))
    table = joined(*lax.all_to_all(tables, "z", 0, 0, tiled=True))

    n_all = 2 * NZ * n_rows
    packed, log_norm = call(
        functools.partial(spread_kernel, [o for o, *_ in groups]),
        (
            shape((N_OWNERS, owned * feat_dim // LANES + EXTRA, LANES)),
            shape((1, LANES)),
        ),
        (
            *(group[2] for group in groups),
            *(group[3] for group in groups),
            *(group[1] for group in groups),
            table,
        ),
        "spread",
        4 * local_count * n_all * feat_dim,
        2 * local_count * n_all,
    )
    came = lax.all_to_all(packed.astype(jnp.float16), OWNERS, 0, 0, tiled=True)
    updated, counts = call(
        update_kernel,
        (shape((owned, feat_dim)), shape((1, owned))),
        (came.astype(jnp.float32), owned_cents),
        "update",
    )
    return (updated, counts.reshape(-1), log_norm.reshape(-1))


def solution(mesh):
    split = Mesh(mesh.devices.reshape(2, NZ, 2, 4, 2), AXES)
    block = ("x_lo", "z", "core")
    return jax.shard_map(
        local,
        mesh=split,
        in_specs=(P(AXES, None), P(block, None), P(block)),
        out_specs=(P(AXES, None), P(AXES), P(AXES)),
        check_vma=False,
    )
```
